256 devices in a mesh: sfc: 256 (over y, z, x, core).
Axes of the slice: x: 4, y: 4, z: 8, core: 2. Of those that a mesh axis runs over, the one named last changes fastest.
Arguments:
- fraction: float32 [2048, 4096], P('sfc'), may hold values from 0 to 1
- centroid: float32 [2048, 3, 4096], P('sfc'), may hold values from -0.5 to 0.5
- velocity: float32 [2048, 3, 4096], P('sfc'), may hold values from -4 to 4
- neighbours: int32 [2048, 6], P('sfc'), may hold values from -1 to 2047, as said below
- refinement: int32 [4096, 4], P('sfc'), may hold values from -1 to 2047, as said below
Outputs:
- planes: float32 [2048, 4, 4096], P('sfc')
- reflux: float32 [2048, 6, 2, 256], P('sfc')
The draws below stay inside these ranges and needn't reach their ends.
Inputs may be any that keep to these rules, and one draw needn't show every extreme that they name: `neighbours`: -1 marks the domain boundary; any other entry is a block on a device at most 2 away along the curve. `refinement`: each row is fine block, direction 0 to 5, coarse block, quadrant 0 to 3. A fine block of -1 marks an empty slot and a device's live slots come first; a live fine block is held by the device that holds the row; the coarse block lies on a device at most 2 away along the curve; every device has a live slot and some device has all 16 live.
All inputs are finite; a program needn't handle non-finite values.
Results may differ from the reference program's by a relative error of at most 0.0003.
Values sent between devices are 32-bit elements; how exact they have to be, the bound alone decides.
No kernel may reach another device: no remote copies, remote signals or barrier semaphores. Data moves between devices by JAX's collectives and lax.ppermute only.
A program may use at most 64 MiB of HBM per device.

```python
import jax
import jax.numpy as jnp
from jax import lax

EDGE = 16
CELLS = 4096
FACE = 256
BLK = 8
REF_DEV = 16
REACH = 2
PASSES = 6
NB = 2048
NREF = 4096
N_SFC = 256


def draw_neighbours(key, part):
    devices = NB // BLK
    subkeys = jax.random.split(jax.random.fold_in(key, 11), 3)
    block_ids = jnp.arange(NB, dtype=jnp.int32)[:, None]
    direction_ids = jnp.arange(6, dtype=jnp.int32)[None, :]
    device_of = block_ids // BLK
    step_dev = jax.random.randint(subkeys[0], (NB, 6), -REACH, REACH + 1)
    target_dev = jnp.clip(device_of + step_dev, 0, devices - 1)
    local_slot = jax.random.randint(subkeys[1], (NB, 6), 0, BLK)
    chosen = target_dev * BLK + local_slot
    boundary = jax.random.randint(subkeys[2], (NB, 6), 0, 16) == 0
    chosen = jnp.where(boundary, -1, chosen)
    chosen = jnp.where((block_ids == 0) & (direction_ids == 0), -1, chosen)
    chosen = jnp.where((block_ids == NB - 1) & (direction_ids == 1), NB - 1, chosen)
    return chosen.astype(jnp.int32)


def draw_refinement(key, part):
    devices = NREF // REF_DEV
    subkeys = jax.random.split(jax.random.fold_in(key, 23), 7)
    slot_ids = jnp.arange(NREF, dtype=jnp.int32)
    device_of = slot_ids // REF_DEV
    within = slot_ids % REF_DEV
    counts = jax.random.randint(subkeys[0], (devices,), REF_DEV // 4 + 1, REF_DEV * 5 // 8 + 1)
    full_device = jax.random.randint(subkeys[1], (), 0, devices)
    counts = jnp.where(jnp.arange(devices, dtype=jnp.int32) == full_device, REF_DEV, counts)
    live = within < counts[device_of]
    fine = jnp.where(live, device_of * BLK + jax.random.randint(subkeys[2], (NREF,), 0, BLK), -1)
    direction = jax.random.randint(subkeys[3], (NREF,), 0, 6)
    coarse_dev = jnp.clip(device_of + jax.random.randint(subkeys[4], (NREF,), -REACH, REACH + 1), 0, devices - 1)
    coarse = coarse_dev * BLK + jax.random.randint(subkeys[5], (NREF,), 0, BLK)
    coarse = jnp.where(slot_ids == NREF - 1, devices * BLK - 1, coarse)
    quadrant = jax.random.randint(subkeys[6], (NREF,), 0, 4)
    return jnp.stack([fine, direction, coarse, quadrant], axis=1).astype(jnp.int32)


def level_of(own_key, dims, cuts, low, top_value):
    loudness, own = 1.0, jax.random.fold_in(own_key, 6)
    for axis_at, blocks in cuts:
        heights = jnp.exp(jax.random.uniform(jax.random.fold_in(own, axis_at), (blocks,), jnp.float32, low / len(cuts), top_value / len(cuts)))
        loudness = loudness * jnp.repeat(heights, dims[axis_at] // blocks).reshape([-1 if axis == axis_at else 1 for axis in range(len(dims))])
    return loudness


def bell_draw(key, extent, width, bound, cuts=(), held_as=jnp.bfloat16):
    loudness = level_of(key, extent, cuts, -0.22, 0.18) if cuts else 1.0
    drawn = jax.random.normal(key, extent, jnp.float32) * width * loudness
    return jnp.minimum(jnp.maximum(drawn, -bound), bound).astype(held_as)


def setup_inputs(seed: int = 0) -> dict:
    seeds = jax.random.split(jax.random.key(seed), 6)
    fraction = jnp.clip(1.0 * jax.random.uniform(seeds[0], (NB, CELLS), jnp.float32) ** level_of(seeds[0], (NB, CELLS), ((0, 256),), -0.2, 0.2), 0.0, 1.0)
    centroid = jnp.clip(jax.random.uniform(seeds[1], (NB, 3, CELLS), jnp.float32, -0.5, 0.5) * level_of(seeds[1], (NB, 3, CELLS), ((0, 256),), -0.4, 0.0), -0.5, 0.5)
    velocity = bell_draw(seeds[2], (NB, 3, CELLS), 1.0, 4.0, ((0, 256),), jnp.float32)
    neighbours = draw_neighbours(jax.random.fold_in(seeds[5], 71), 0)
    refinement = draw_refinement(jax.random.fold_in(seeds[5], 71), 0)
    return {"fraction": fraction, "centroid": centroid, "velocity": velocity, "neighbours": neighbours, "refinement": refinement}


time_step = 0.25
damping = 0.1

def faces_of(values):
    leading = values.shape[:-1]
    blocks_cube = values.reshape(leading + (EDGE, EDGE, EDGE))
    layers = [blocks_cube[..., 0, :, :], blocks_cube[..., EDGE - 1, :, :], blocks_cube[..., :, 0, :], blocks_cube[..., :, EDGE - 1, :], blocks_cube[..., :, :, 0], blocks_cube[..., :, :, EDGE - 1]]
    return jnp.stack([face_layer.reshape(leading + (EDGE * EDGE,)) for face_layer in layers], axis=len(leading) - 1)

def opposite_of(direction):
    return direction + 1 - 2 * (direction % 2)

def neighbour_fields(own_cells, ghost_faces):
    count_blocks, fields = (own_cells.shape[0], own_cells.shape[1])
    blocks_cube = own_cells.reshape(count_blocks, fields, EDGE, EDGE, EDGE)
    ghost_cube = ghost_faces.reshape(count_blocks, 6, fields, EDGE, EDGE)
    minus_x = jnp.concatenate([ghost_cube[:, 0][:, :, None], blocks_cube[:, :, :-1]], 2)
    plus_x = jnp.concatenate([blocks_cube[:, :, 1:], ghost_cube[:, 1][:, :, None]], 2)
    minus_y = jnp.concatenate([ghost_cube[:, 2][:, :, :, None], blocks_cube[:, :, :, :-1]], 3)
    plus_y = jnp.concatenate([blocks_cube[:, :, :, 1:], ghost_cube[:, 3][:, :, :, None]], 3)
    minus_z = jnp.concatenate([ghost_cube[:, 4][..., None], blocks_cube[..., :-1]], 4)
    plus_z = jnp.concatenate([blocks_cube[..., 1:], ghost_cube[:, 5][..., None]], 4)
    return [field.reshape(count_blocks, fields, -1) for field in (minus_x, plus_x, minus_y, plus_y, minus_z, plus_z)]

def cholesky_solve(matrix, vector):
    order_size = len(vector)
    lower = [[None] * order_size for _unused in range(order_size)]
    for row_index in range(order_size):
        for column_index in range(row_index + 1):
            running = matrix[row_index][column_index]
            for middle in range(column_index):
                running = running - lower[row_index][middle] * lower[column_index][middle]
            if row_index == column_index:
                lower[row_index][row_index] = jnp.sqrt(running)
            else:
                lower[row_index][column_index] = running / lower[column_index][column_index]
    forward = []
    for row_index in range(order_size):
        running = vector[row_index]
        for middle in range(row_index):
            running = running - lower[row_index][middle] * forward[middle]
        forward.append(running / lower[row_index][row_index])
    result = [None] * order_size
    for row_index in reversed(range(order_size)):
        running = forward[row_index]
        for middle in range(row_index + 1, order_size):
            running = running - lower[middle][row_index] * result[middle]
        result[row_index] = running / lower[row_index][row_index]
    return result

def fit_planes(center, neighbours_list):
    frac_center = center[:, 0]
    points = [(center[:, 1], center[:, 2], center[:, 3], frac_center)]
    for direction in range(6):
        axis_index = direction // 2
        offset = 2.0 * (direction % 2) - 1.0
        values = neighbours_list[direction]
        coords = [values[:, 1], values[:, 2], values[:, 3]]
        coords[axis_index] = coords[axis_index] + offset
        points.append((coords[0], coords[1], coords[2], values[:, 0]))
    params = [2.0 * (neighbours_list[2 * axis_index + 1][:, 0] - neighbours_list[2 * axis_index][:, 0]) for axis_index in range(3)]
    params.append(2.0 * (2.0 * frac_center - 1.0) - params[0] * center[:, 1] - params[1] * center[:, 2] - params[2] * center[:, 3])
    for _unused in range(PASSES):
        jacobian = []
        residual = []
        for point in points:
            phase = params[0] * point[0] + params[1] * point[1] + params[2] * point[2] + params[3]
            tanh_value = jnp.tanh(phase)
            residual.append(0.5 * (1.0 + tanh_value) - point[3])
            slope = 0.5 * (1.0 - tanh_value * tanh_value)
            jacobian.append([slope * point[0], slope * point[1], slope * point[2], slope])
        matrix = [[sum((row_entry[first_index] * row_entry[second_index] for row_entry in jacobian)) + (damping if first_index == second_index else 0.0) for second_index in range(4)] for first_index in range(4)]
        vector = [sum((jacobian[point_index][first_index] * residual[point_index] for point_index in range(7))) for first_index in range(4)]
        update = cholesky_solve(matrix, vector)
        params = [params[index_value] - update[index_value] for index_value in range(4)]
    return jnp.stack(params, axis=1)

def build_plane_faces(planes, velocity):
    coef_faces = faces_of(planes)
    speed_faces = faces_of(velocity)
    normal_speed = jnp.stack([speed_faces[:, direction, direction // 2] for direction in range(6)], axis=1)
    return jnp.concatenate([coef_faces, normal_speed[:, :, None]], 2)

def pick_component(coefs, which):
    picked = jnp.zeros_like(coefs[:, 0])
    for axis_index in range(3):
        picked = picked + (which[:, None] == axis_index).astype(coefs.dtype) * coefs[:, axis_index]
    return picked

def slot_moments(fine_face, coarse_face, direction, quadrant, live):
    face_index = jnp.arange(EDGE * EDGE, dtype=jnp.int32)
    first_pos = face_index // EDGE
    second_pos = face_index % EDGE
    half_edge = EDGE // 2
    coarse_cell = ((quadrant // 2)[:, None] * half_edge + first_pos[None] // 2) * EDGE + (quadrant % 2)[:, None] * half_edge + second_pos[None] // 2
    mapped = jnp.take_along_axis(coarse_face, coarse_cell[:, None, :], axis=2)
    axis_index = direction // 2
    first_tangent = jnp.where(axis_index == 0, 1, 0)
    second_tangent = jnp.where(axis_index == 2, 1, 2)
    sign = (2 * (direction % 2) - 1).astype(fine_face.dtype)[:, None]
    normal_fine = pick_component(fine_face, axis_index)
    normal_coarse = pick_component(mapped, axis_index)
    tangent_one = pick_component(mapped, first_tangent)
    tangent_two = pick_component(mapped, second_tangent)
    offset_one = ((first_pos % 2).astype(fine_face.dtype) - 0.5) * 0.5
    offset_two = ((second_pos % 2).astype(fine_face.dtype) - 0.5) * 0.5
    speed = sign * 0.5 * (fine_face[:, 4] + mapped[:, 4])
    depth = jnp.abs(speed) * time_step
    outflow = jnp.maximum(speed, 0.0)
    inflow = jnp.minimum(speed, 0.0)
    volume = jnp.zeros_like(speed)
    moment = jnp.zeros_like(speed)
    for node in (0.5 - 3.0 ** 0.5 / 6.0, 0.5 + 3.0 ** 0.5 / 6.0):
        fine_phase = normal_fine * (sign * (0.5 - node * depth)) + fine_face[:, 3]
        coarse_phase = normal_coarse * (-sign * (0.5 - 0.5 * node * depth)) + tangent_one * offset_one + tangent_two * offset_two + mapped[:, 3]
        fine_model = 0.5 * (1.0 + jnp.tanh(fine_phase))
        coarse_model = 0.5 * (1.0 + jnp.tanh(coarse_phase))
        volume = volume + 0.5 * time_step * (outflow * fine_model + inflow * coarse_model)
        moment = moment + 0.5 * time_step * node * depth * sign * (inflow * coarse_model - outflow * fine_model)
    weight = live.astype(fine_face.dtype)[:, None]
    return (jnp.stack([volume * weight, moment * weight], axis=1), coarse_cell)

def fit_group(group):
    center, ghosts = group
    return fit_planes(center, neighbour_fields(center, ghosts))

def reference(fraction, centroid, velocity, neighbours, refinement):
    own = jnp.concatenate([fraction[:, None], centroid], 1)
    own_faces = faces_of(own)
    opposite = opposite_of(jnp.arange(6, dtype=jnp.int32))
    safe = jnp.clip(neighbours, 0, NB - 1)
    ghost = jnp.where((neighbours >= 0)[:, :, None, None], own_faces[safe, opposite[None, :]], own_faces)
    grouped = lax.map(fit_group, (own.reshape(N_SFC, BLK, 4, CELLS), ghost.reshape(N_SFC, BLK, 6, 4, FACE)))
    planes = grouped.reshape(NB, 4, CELLS)
    plane_faces = build_plane_faces(planes, velocity)
    fine = refinement[:, 0]
    live = fine >= 0
    direction = refinement[:, 1]
    coarse = refinement[:, 2]
    quadrant = refinement[:, 3]
    fine_face = plane_faces[jnp.clip(fine, 0, NB - 1), direction]
    coarse_face = plane_faces[coarse, opposite_of(direction)]
    moments, coarse_cell = slot_moments(fine_face, coarse_face, direction, quadrant, live)
    target = (coarse * 6 + opposite_of(direction))[:, None] * FACE + coarse_cell
    flat = jnp.zeros((NB * 6 * FACE, 2), jnp.float32).at[target.reshape(-1)].add(jnp.swapaxes(moments, 1, 2).reshape(-1, 2))
    reflux = jnp.swapaxes(flat.reshape(NB, 6, FACE, 2), 2, 3)
    return (planes, reflux)
```

```python
import functools

import jax
import jax.numpy as jnp
from jax import lax
from jax.experimental import pallas as pl
from jax.experimental.pallas import tpu as pltpu
from jax.sharding import PartitionSpec as P

BLK = 8
SLOTS = 16
PASSES = 6
LANES = 128
GROUP = 4
NODES = (0.5 - 3.0**0.5 / 6.0, 0.5 + 3.0**0.5 / 6.0)
TIME_STEP = 0.25
DAMPING = 0.1
VMEM_SPEC = pl.BlockSpec(memory_space=pltpu.VMEM)
SMEM_SPEC = pl.BlockSpec(memory_space=pltpu.SMEM)


def lane_ids():
    return lax.broadcasted_iota(jnp.int32, (8, LANES), 1)


def row_ids():
    return lax.broadcasted_iota(jnp.int32, (8, LANES), 0)


def pick(values, index):
    return jnp.take_along_axis(values, index, axis=1, mode="promise_in_bounds")


def cells(ref, b, xh, yh):
    return ref[pl.ds(xh * 128 + yh * 8 + b, 8, stride=16), :]


def side_index(lane):
    l = lane % 64
    index = jnp.where(l < 16, l, jnp.where(l < 32, l + 96, 16 * (l % 8) + jnp.where(l < 48, 0, 15)))
    upper = ((l >= 16) & (l < 32)) | ((l >= 40) & (l < 48)) | (l >= 56)
    return index, upper


def pack_kernel(frac_ref, cent_ref, refine_ref, out_ref):
    lane = lane_ids()
    index, upper = side_index(lane)

    def block(b, carry):
        for xh in (0, 1):
            sides = []
            for f in range(4):
                ref = frac_ref if f == 0 else cent_ref.at[f - 1]
                half = [cells(ref, b, xh, yh) for yh in (0, 1)]
                for yh in (0, 1):
                    row = half[yh][0:1] if xh == 0 else half[yh][7:8]
                    out_ref[b * 6 + xh, 2 * f + yh : 2 * f + yh + 1, :] = row
                sides.append(jnp.where(upper, pick(half[1], index), pick(half[0], index)))
            for fp in (0, 1):
                out_ref[b * 6 + 2 + 2 * fp + xh] = jnp.where(lane < 64, sides[2 * fp], sides[2 * fp + 1])
        return carry

    lax.fori_loop(0, BLK, block, 0)
    out_ref[48] = jnp.zeros((8, LANES), jnp.float32)
    table = refine_ref[...].astype(jnp.float32)
    out_ref[48, :, 0:4] = table[0:8]
    out_ref[48, :, 4:8] = table[8:16]


def solve(h, g):
    a, b, c = h[0][0], h[0][1], h[1][1]
    ra = 1.0 / (a * c - b * b)
    ia, ib, ic = c * ra, b * ra, a * ra
    p, q, r, s = h[0][2], h[0][3], h[1][2], h[1][3]
    wp, wq = ia * p - ib * r, ia * q - ib * s
    wr, ws = ic * r - ib * p, ic * s - ib * q
    sa = h[2][2] - p * wp - r * wr
    sb = h[2][3] - p * wq - r * ws
    sc = h[3][3] - q * wq - s * ws
    z0, z1 = ia * g[0] - ib * g[1], ic * g[1] - ib * g[0]
    y0 = g[2] - p * z0 - r * z1
    y1 = g[3] - q * z0 - s * z1
    rs = 1.0 / (sa * sc - sb * sb)
    x2 = (sc * y0 - sb * y1) * rs
    x3 = (sa * y1 - sb * y0) * rs
    return z0 - wp * x2 - wq * x3, z1 - wr * x2 - ws * x3, x2, x3


def one_pass(load, params):
    a, b, c, d = params
    h = [[None] * 4 for _ in range(4)]
    g = [None] * 4

    def add(total, value):
        return value if total is None else total + value

    for j in range(7):
        px, py, pz, q = load(j)
        t = jnp.tanh(a * px + b * py + c * pz + d)
        s = 1.0 - t * t
        w = s * s
        r = s * (t + q)
        wx, wy, wz = w * px, w * py, w * pz
        h[0][0] = add(h[0][0], wx * px)
        h[0][1] = add(h[0][1], wx * py)
        h[0][2] = add(h[0][2], wx * pz)
        h[0][3] = add(h[0][3], wx)
        h[1][1] = add(h[1][1], wy * py)
        h[1][2] = add(h[1][2], wy * pz)
        h[1][3] = add(h[1][3], wy)
        h[2][2] = add(h[2][2], wz * pz)
        h[2][3] = add(h[2][3], wz)
        h[3][3] = add(h[3][3], w)
        g[0] = add(g[0], r * px)
        g[1] = add(g[1], r * py)
        g[2] = add(g[2], r * pz)
        g[3] = add(g[3], r)
    for i in range(4):
        h[i][i] = h[i][i] + 4.0 * DAMPING
    step = solve(h, g)
    return tuple(p - u for p, u in zip(params, step))


def start(load):
    f = [0.5 - 0.5 * load(j)[3] for j in range(7)]
    cx, cy, cz, _ = load(0)
    a, b, c = (2.0 * (f[2 * k + 2] - f[2 * k + 1]) for k in range(3))
    d = 2.0 * (2.0 * f[0] - 1.0) - a * cx - b * cy - c * cz
    return a, b, c, d


def stencil(tbl_ref, frac_ref, cent_ref, table, xpad, st):
    lane = lane_ids()
    spread_z = [
        [fh * 64 + jnp.where(lane % 16 == 15, 32, 48) + yh * 8 + lane // 16 for yh in (0, 1)]
        for fh in (0, 1)
    ]
    spread_y = [[fh * 64 + (16 if yh == 0 else 0) + lane % 16 for yh in (0, 1)] for fh in (0, 1)]
    group = (lane % 64) // 16

    def block(b, carry):
        src = [tbl_ref[b * 6 + k] for k in range(6)]
        low, high = table[src[0]], table[src[1]]
        for f in range(4):
            ref = frac_ref if f == 0 else cent_ref.at[f - 1]

            def put(j, xh, yh, value):
                if f == 0:
                    st[j, 3, pl.ds(b * 32 + (xh * 2 + yh) * 8, 8), :] = 1.0 - 2.0 * value
                else:
                    if j > 0 and (j - 1) // 2 == f - 1:
                        value = value + (1.0 if (j - 1) % 2 else -1.0)
                    st[j, f - 1, pl.ds(b * 32 + (xh * 2 + yh) * 8, 8), :] = value

            own = [[cells(ref, b, xh, yh) for yh in (0, 1)] for xh in (0, 1)]
            for yh in (0, 1):
                xpad[f, yh, 7:8, :] = low[2 * f + yh : 2 * f + yh + 1]
                xpad[f, yh, 24:25, :] = high[2 * f + yh : 2 * f + yh + 1]
                for xh in (0, 1):
                    xpad[f, yh, 8 + 8 * xh : 16 + 8 * xh, :] = own[xh][yh]
            for xh in (0, 1):
                ghost = [table[src[k] + 2 * (f // 2) + xh] for k in range(2, 6)]
                mixed = jnp.where(
                    group < 2,
                    jnp.where(group == 0, ghost[1], ghost[0]),
                    jnp.where(group == 2, ghost[3], ghost[2]),
                )
                up = [pltpu.roll(own[xh][yh], 16, 1) for yh in (0, 1)]
                down = [pltpu.roll(own[xh][yh], LANES - 16, 1) for yh in (0, 1)]
                gy = [pick(mixed, spread_y[f % 2][yh]) for yh in (0, 1)]
                for yh in (0, 1):
                    mine = own[xh][yh]
                    gz = pick(mixed, spread_z[f % 2][yh])
                    put(0, xh, yh, mine)
                    put(1, xh, yh, xpad[f, yh, 7 + 8 * xh : 15 + 8 * xh, :])
                    put(2, xh, yh, xpad[f, yh, 9 + 8 * xh : 17 + 8 * xh, :])
                    put(3, xh, yh, jnp.where(lane < 16, gy[0] if yh == 0 else up[0], up[yh]))
                    put(4, xh, yh, jnp.where(lane >= 112, gy[1] if yh == 1 else down[1], down[yh]))
                    put(5, xh, yh, jnp.where(lane % 16 == 0, gz, pltpu.roll(mine, 1, 1)))
                    put(6, xh, yh, jnp.where(lane % 16 == 15, gz, pltpu.roll(mine, LANES - 1, 1)))
        return carry

    lax.fori_loop(0, BLK, block, 0)


def plane_faces(velo_ref, params, pf):
    lane = lane_ids()
    row = row_ids()
    l = lane % 128
    index = jnp.where(
        l < 48, l % 16, jnp.where(l < 64, l + 64, 16 * (l % 8) + jnp.where(l < 80, 0, 15))
    )
    upper = ((l >= 48) & (l < 64)) | ((l >= 72) & (l < 80)) | ((l >= 88) & (l < 96))
    unroll_x = row * 16 + lane % 16

    def block(b, carry):
        def face(first, second, third):
            for h in (0, 1):
                low = pick(jnp.broadcast_to(first[0][h][0:1], (8, LANES)), unroll_x)
                high = pick(jnp.broadcast_to(first[1][h][7:8], (8, LANES)), unroll_x)
                if second is third:
                    zero, one = second[h]
                else:
                    zero = second[h][0], third[h][0]
                    one = second[h][1], third[h][1]
                if second is third:
                    sides = jnp.where(upper, pick(one, index), pick(zero, index))
                else:
                    sides = jnp.where(
                        l < 64,
                        jnp.where(upper, pick(one[0], index), pick(zero[0], index)),
                        jnp.where(upper, pick(one[1], index), pick(zero[1], index)),
                    )
                yield h, jnp.where(l < 16, low, jnp.where(l < 32, high, sides))

        for comp in range(4):
            value = [
                [params[comp, pl.ds(b * 32 + (xh * 2 + yh) * 8, 8), :] for yh in (0, 1)]
                for xh in (0, 1)
            ]
            for h, packed in face(value, value, value):
                pf[b * 5 + comp, 8 * h : 8 * h + 8, :] = packed
        speed = [
            [[cells(velo_ref.at[axis], b, xh, yh) for yh in (0, 1)] for xh in (0, 1)]
            for axis in range(3)
        ]
        for h, packed in face(*speed):
            pf[b * 5 + 4, 8 * h : 8 * h + 8, :] = packed
        return carry

    lax.fori_loop(0, BLK, block, 0)


def fine_slots(refine_ref, pf, slots):
    lane = lane_ids()

    def slot(s, carry):
        f = refine_ref[s * 2]
        k = refine_ref[s * 2 + 1]
        index = k * 16 + 2 * (lane % 8) + (lane // 8) % 2
        odd = (lane // 16) % 2 == 1
        parts = []
        for comp in (lax.shift_right_logical(k, 1), 3, 4):
            even_rows = pf[f * 5 + comp, pl.ds(0, 8, stride=2), :]
            odd_rows = pf[f * 5 + comp, pl.ds(1, 8, stride=2), :]
            parts.append(jnp.where(odd, pick(odd_rows, index), pick(even_rows, index)))
        slots[s] = jnp.where(lane < 32, parts[0], jnp.where(lane < 64, parts[1], parts[2]))
        return carry

    lax.fori_loop(0, SLOTS, slot, 0)


def fit_kernel(
    tbl_ref, refine_ref, own_ref, r1_ref, r2_ref, r3_ref, r4_ref, frac_ref, cent_ref, velo_ref,
    planes_ref, pf_ref, slots_ref, table, xpad, st, params,
):
    lane = lane_ids()
    for at, ref in enumerate((own_ref, r1_ref, r2_ref, r3_ref, r4_ref)):

        def copy(i, carry, at=at, ref=ref):
            for u in range(6):
                table[at * 48 + i * 6 + u] = ref[i * 6 + u]
            return carry

        lax.fori_loop(0, BLK, copy, 0)

    def swap(i, carry):
        for u in range(2, 6):
            v = own_ref[i * 6 + u]
            odd = (lane // 16) % 2 == 1
            table[240 + i * 6 + u] = jnp.where(
                odd, pltpu.roll(v, 16, 1), pltpu.roll(v, LANES - 16, 1)
            )
        return carry

    lax.fori_loop(0, BLK, swap, 0)
    stencil(tbl_ref, frac_ref, cent_ref, table, xpad, st)

    rows = GROUP * 8

    def fit(i, carry):
        at = pl.ds(pl.multiple_of(i * rows, rows), rows)

        def load(j):
            return tuple(st[j, c, at, :] for c in range(4))

        values = lax.fori_loop(0, PASSES, lambda _, p: one_pass(load, p), start(load))
        for comp in range(4):
            params[comp, at, :] = values[comp]
        return carry

    lax.fori_loop(0, 32 // GROUP, fit, 0)

    def emit(b, carry):
        for comp in range(4):
            for xh in (0, 1):
                for yh in (0, 1):
                    planes_ref[pl.ds(b * 128 + 64 * xh + 4 * yh + comp, 8, stride=8), :] = params[
                        comp, pl.ds(b * 32 + (xh * 2 + yh) * 8, 8), :
                    ]
        return carry

    lax.fori_loop(0, BLK, emit, 0)
    plane_faces(velo_ref, params, pf_ref)
    fine_slots(refine_ref, pf_ref, slots_ref)


def moment_kernel(
    meta_ref, pf_ref, s0_ref, s1_ref, s2_ref, s3_ref, s4_ref, out_ref, slots, todo
):
    lane = lane_ids()
    row = row_ids()
    out_ref[...] = jnp.zeros_like(out_ref)
    for at, ref in enumerate((s0_ref, s1_ref, s2_ref, s3_ref, s4_ref)):
        for u in range(SLOTS):
            slots[at * SLOTS + u] = ref[u]
    total = 5 * SLOTS

    def collect(i, n):
        todo[n] = i
        return n + meta_ref[i * 4]

    count = lax.fori_loop(0, total, collect, 0)
    for extra in range(4):
        todo[count + extra] = 0
    quarter = lane // 32
    first_off = (((lane // 16) % 2).astype(jnp.float32) - 0.5) * 0.5
    second_off = (((lane // 8) % 2).astype(jnp.float32) - 0.5) * 0.5

    def group(g, carry):
        fine = [None] * 3
        coarse = [None] * 5
        sign = None
        weight = None
        where = []

        def merge(old, new, q):
            return new if old is None else jnp.where(quarter == q, new, old)

        for q in range(4):
            at = 4 * g + q
            i = todo[at]
            c = meta_ref[i * 4 + 1]
            k = meta_ref[i * 4 + 2]
            quad = meta_ref[i * 4 + 3]
            axis = lax.shift_right_logical(k, 1)
            qa = lax.shift_right_logical(quad, 1)
            qb = quad & 1
            source = slots[i]
            for comp in range(3):
                turn = ((q - comp) * 32) % LANES
                moved = source if turn == 0 else pltpu.roll(source, turn, 1)
                fine[comp] = merge(fine[comp], moved, q)
            index = k * 16 + qb * 8 + lane % 8
            which = (axis, jnp.where(axis == 0, 1, 0), jnp.where(axis == 2, 1, 2), 3, 4)
            for at_comp, comp in enumerate(which):
                value = pf_ref[c * 5 + comp, pl.ds(pl.multiple_of(qa * 8, 8), 8), :]
                coarse[at_comp] = merge(coarse[at_comp], pick(value, index), q)
            s = jnp.where((k & 1) == 1, -1.0, 1.0).astype(jnp.float32)
            sign = merge(sign, jnp.full((8, LANES), s, jnp.float32), q)
            on = jnp.where(at < count, 1.0, 0.0).astype(jnp.float32)
            weight = merge(weight, jnp.full((8, LANES), on, jnp.float32), q)
            where.append((((c * 6 + k) * 2 + qa) * 2, qb))
        an, df, uf = fine
        cn, t1, t2, dc, uc = coarse
        speed = sign * 0.5 * (uf + uc)
        depth = jnp.abs(speed) * TIME_STEP
        outflow = jnp.maximum(speed, 0.0)
        inflow = jnp.minimum(speed, 0.0)
        base = t1 * first_off + t2 * second_off + dc
        volume = 0.0
        moment = 0.0
        for node in NODES:
            fine_phase = an * (sign * (0.5 - node * depth)) + df
            coarse_phase = cn * (-sign * (0.5 - 0.5 * node * depth)) + base
            fine_model = 0.5 * (1.0 + jnp.tanh(fine_phase))
            coarse_model = 0.5 * (1.0 + jnp.tanh(coarse_phase))
            gain = outflow * fine_model
            loss = inflow * coarse_model
            volume = volume + 0.5 * TIME_STEP * (gain + loss)
            moment = moment + 0.5 * TIME_STEP * node * depth * sign * (loss - gain)
        sums = []
        for value in (volume * weight, moment * weight):
            value = value + pltpu.roll(value, LANES - 8, 1)
            sums.append(value + pltpu.roll(value, LANES - 16, 1))
        for q in range(4):
            target, qb = where[q]
            index = 32 * q + lane % 8
            keep = (lane // 16 == row) & ((lane // 8) % 2 == qb)
            rows = [
                jnp.sum(jnp.where(keep, pick(value, index), 0.0), axis=0, keepdims=True)
                for value in sums
            ]
            for m in range(2):
                out_ref[pl.ds(target + m, 1), :] = out_ref[pl.ds(target + m, 1), :] + rows[m]
        return carry

    lax.fori_loop(0, (count + 3) // 4, group, 0)


def partners(n, distance, offset):
    pairs = []
    for i in range(n):
        up = ((i - offset) // distance) % 2 == 0
        pairs.append((i, (i + distance if up else i - distance) % n))
    return pairs


def trade(value):
    n = lax.axis_size("sfc")
    return [
        lax.ppermute(value, "sfc", partners(n, distance, offset))
        for distance, offset in ((1, 0), (1, 1), (2, 0), (2, 2))
    ]


def tiles(field):
    return field.reshape(BLK, 32, LANES).transpose(1, 0, 2).reshape(256, LANES)


def tiles3(field):
    return field.reshape(BLK, 3, 32, LANES).transpose(1, 2, 0, 3).reshape(3, 256, LANES)


def per_device(fraction, centroid, velocity, neighbours, refinement):
    f32 = jnp.float32
    i32 = jnp.int32
    me = lax.axis_index("sfc").astype(i32)
    frac, cent, velo = tiles(fraction), tiles3(centroid), tiles3(velocity)
    out = functools.partial(jax.ShapeDtypeStruct, dtype=f32)
    limit = pltpu.CompilerParams(vmem_limit_bytes=48 << 20)

    faces = pl.pallas_call(
        pack_kernel,
        out_shape=out((49, 8, LANES)),
        in_specs=[VMEM_SPEC] * 3,
        out_specs=VMEM_SPEC,
        compiler_params=limit,
        name="pack",
    )(frac, cent, refinement)
    got = trade(faces)

    offset = neighbours // BLK - me
    odd = me % 2
    odd2 = (me // 2) % 2
    near = jnp.where(offset == 1 - 2 * odd, 1, 2)
    far = jnp.where(offset == 2 - 4 * odd2, 3, 4)
    part = jnp.where(offset == 0, 0, jnp.where(jnp.abs(offset) == 1, near, far))
    direction = jnp.arange(6, dtype=i32)[None, :]
    block = jnp.arange(BLK, dtype=i32)[:, None]
    inside = part * BLK + neighbours % BLK
    x_row = jnp.where(neighbours >= 0, inside * 6 + 1 - direction, block * 6 + direction)
    yz_row = jnp.where(neighbours >= 0, inside, 40 + block) * 6 + 2
    rows = jnp.where(direction < 2, x_row, yz_row)
    rows = jnp.clip(rows, 0, 285).reshape(48)

    fine_local = jnp.clip(refinement[:, 0] - me * BLK, 0, BLK - 1)
    fine_side = jnp.clip(refinement[:, 1], 0, 5)
    fine_table = jnp.stack([fine_local, fine_side], axis=1).reshape(2 * SLOTS)

    planes, plane_face, slots = pl.pallas_call(
        fit_kernel,
        out_shape=(out((1024, LANES)), out((BLK * 5, 16, LANES)), out((SLOTS, 8, LANES))),
        in_specs=[SMEM_SPEC] * 2 + [VMEM_SPEC] * 8,
        out_specs=(VMEM_SPEC,) * 3,
        scratch_shapes=[
            pltpu.VMEM((288, 8, LANES), f32),
            pltpu.VMEM((4, 2, 32, LANES), f32),
            pltpu.VMEM((7, 4, 256, LANES), f32),
            pltpu.VMEM((4, 256, LANES), f32),
        ],
        compiler_params=limit,
        name="fit",
    )(rows, fine_table, faces, *got, frac, cent, velo)

    got_slots = trade(slots)
    tables = [refinement] + [
        jnp.concatenate([v[48, :, 0:4], v[48, :, 4:8]], axis=0).astype(i32) for v in got
    ]
    table = jnp.concatenate(tables, axis=0)
    mine = (table[:, 0] >= 0) & (table[:, 2] // BLK == me)
    side = jnp.clip(table[:, 1], 0, 5)
    meta = jnp.stack(
        [
            mine.astype(i32),
            jnp.clip(table[:, 2], 0, None) % BLK,
            side + 1 - 2 * (side % 2),
            jnp.clip(table[:, 3], 0, 3),
        ],
        axis=1,
    ).reshape(4 * 5 * SLOTS)

    reflux = pl.pallas_call(
        moment_kernel,
        out_shape=out((BLK * 6 * 4, LANES)),
        in_specs=[SMEM_SPEC] + [VMEM_SPEC] * 6,
        out_specs=VMEM_SPEC,
        scratch_shapes=[
            pltpu.VMEM((5 * SLOTS, 8, LANES), f32),
            pltpu.SMEM((5 * SLOTS + 8,), i32),
        ],
        compiler_params=limit,
        name="moments",
    )(meta, plane_face, slots, *got_slots)

    planes = planes.reshape(BLK, 32, 4, LANES).transpose(0, 2, 1, 3).reshape(BLK, 4, 4096)
    reflux = reflux.reshape(BLK, 6, 2, 2, LANES).transpose(0, 1, 3, 2, 4).reshape(BLK, 6, 2, 256)
    return planes, reflux


def solution(mesh):
    return jax.shard_map(
        per_device,
        mesh=mesh,
        in_specs=(
            P("sfc", None),
            P("sfc", None, None),
            P("sfc", None, None),
            P("sfc", None),
            P("sfc", None),
        ),
        out_specs=(P("sfc", None, None), P("sfc", None, None, None)),
        check_vma=False,
    )
```

```python
import functools

import jax
import jax.numpy as jnp
from jax import lax
from jax.experimental import pallas as pl
from jax.experimental.pallas import tpu as pltpu
from jax.sharding import PartitionSpec as P

BLK = 8
SLOTS = 16
PARTS = 6
PASSES = 6
LANES = 128
GROUP = 4
NODES = (0.5 - 3.0**0.5 / 6.0, 0.5 + 3.0**0.5 / 6.0)
TIME_STEP = 0.25
DAMPING = 0.1
VMEM_SPEC = pl.BlockSpec(memory_space=pltpu.VMEM)
SMEM_SPEC = pl.BlockSpec(memory_space=pltpu.SMEM)


def lane_ids():
    return lax.broadcasted_iota(jnp.int32, (8, LANES), 1)


def row_ids():
    return lax.broadcasted_iota(jnp.int32, (8, LANES), 0)


def pick(values, index):
    return jnp.take_along_axis(values, index, axis=1, mode="promise_in_bounds")


def cells(ref, b, xh, yh):
    return ref[pl.ds(xh * 128 + yh * 8 + b, 8, stride=16), :]


def side_index(lane):
    l = lane % 64
    index = jnp.where(l < 16, l, jnp.where(l < 32, l + 96, 16 * (l % 8) + jnp.where(l < 48, 0, 15)))
    upper = ((l >= 16) & (l < 32)) | ((l >= 40) & (l < 48)) | (l >= 56)
    return index, upper


def pack_kernel(frac_hbm, cent_hbm, refine_hbm, out_ref, field, refine_ref, sems):
    copies = [
        pltpu.make_async_copy(frac_hbm if f == 0 else cent_hbm.at[f - 1], field.at[f], sems.at[f])
        for f in range(4)
    ]
    copies.append(pltpu.make_async_copy(refine_hbm, refine_ref, sems.at[4]))
    for copy in copies:
        copy.start()
    lane = lane_ids()
    index, upper = side_index(lane)
    out_ref[48] = jnp.zeros((8, LANES), jnp.float32)
    for copy in copies:
        copy.wait()
    out_ref[48, 0:4, 0:SLOTS] = refine_ref[...].astype(jnp.float32)

    def block(b, carry):
        for xh in (0, 1):
            sides = []
            for f in range(4):
                half = [cells(field.at[f], b, xh, yh) for yh in (0, 1)]
                for yh in (0, 1):
                    row = half[yh][0:1] if xh == 0 else half[yh][7:8]
                    out_ref[b * 6 + xh, 2 * f + yh : 2 * f + yh + 1, :] = row
                sides.append(jnp.where(upper, pick(half[1], index), pick(half[0], index)))
            for fp in (0, 1):
                out_ref[b * 6 + 2 + 2 * fp + xh] = jnp.where(lane < 64, sides[2 * fp], sides[2 * fp + 1])
        return carry

    lax.fori_loop(0, BLK, block, 0)


def solve(h, g):
    a, b, c = h[0][0], h[0][1], h[1][1]
    ra = 1.0 / (a * c - b * b)
    ia, ib, ic = c * ra, b * ra, a * ra
    p, q, r, s = h[0][2], h[0][3], h[1][2], h[1][3]
    wp, wq = ia * p - ib * r, ia * q - ib * s
    wr, ws = ic * r - ib * p, ic * s - ib * q
    sa = h[2][2] - p * wp - r * wr
    sb = h[2][3] - p * wq - r * ws
    sc = h[3][3] - q * wq - s * ws
    z0, z1 = ia * g[0] - ib * g[1], ic * g[1] - ib * g[0]
    y0 = g[2] - p * z0 - r * z1
    y1 = g[3] - q * z0 - s * z1
    rs = 1.0 / (sa * sc - sb * sb)
    x2 = (sc * y0 - sb * y1) * rs
    x3 = (sa * y1 - sb * y0) * rs
    return z0 - wp * x2 - wq * x3, z1 - wr * x2 - ws * x3, x2, x3


def one_pass(load, params):
    a, b, c, d = params
    h = [[None] * 4 for _ in range(4)]
    g = [None] * 4

    def add(total, value):
        return value if total is None else total + value

    for j in range(7):
        px, py, pz, q = load(j)
        t = jnp.tanh(a * px + b * py + c * pz + d)
        s = 1.0 - t * t
        w = s * s
        r = s * (t + q)
        wx, wy, wz = w * px, w * py, w * pz
        h[0][0] = add(h[0][0], wx * px)
        h[0][1] = add(h[0][1], wx * py)
        h[0][2] = add(h[0][2], wx * pz)
        h[0][3] = add(h[0][3], wx)
        h[1][1] = add(h[1][1], wy * py)
        h[1][2] = add(h[1][2], wy * pz)
        h[1][3] = add(h[1][3], wy)
        h[2][2] = add(h[2][2], wz * pz)
        h[2][3] = add(h[2][3], wz)
        h[3][3] = add(h[3][3], w)
        g[0] = add(g[0], r * px)
        g[1] = add(g[1], r * py)
        g[2] = add(g[2], r * pz)
        g[3] = add(g[3], r)
    for i in range(4):
        h[i][i] = h[i][i] + 4.0 * DAMPING
    step = solve(h, g)
    return tuple(p - u for p, u in zip(params, step))


def start(load):
    f = [0.5 - 0.5 * load(j)[3] for j in range(7)]
    cx, cy, cz, _ = load(0)
    a, b, c = (2.0 * (f[2 * k + 2] - f[2 * k + 1]) for k in range(3))
    d = 2.0 * (2.0 * f[0] - 1.0) - a * cx - b * cy - c * cz
    return a, b, c, d


def stencil(tbl_ref, frac_ref, cent_ref, table, xpad, st):
    lane = lane_ids()
    spread_z = [
        [fh * 64 + jnp.where(lane % 16 == 15, 32, 48) + yh * 8 + lane // 16 for yh in (0, 1)]
        for fh in (0, 1)
    ]
    spread_y = [[fh * 64 + (16 if yh == 0 else 0) + lane % 16 for yh in (0, 1)] for fh in (0, 1)]
    group = (lane % 64) // 16

    def block(b, carry):
        src = [tbl_ref[b * 6 + k] for k in range(6)]
        low, high = table[src[0]], table[src[1]]
        for f in range(4):
            ref = frac_ref if f == 0 else cent_ref.at[f - 1]

            def put(j, xh, yh, value):
                if f == 0:
                    st[j, 3, pl.ds(b * 32 + (xh * 2 + yh) * 8, 8), :] = 1.0 - 2.0 * value
                else:
                    if j > 0 and (j - 1) // 2 == f - 1:
                        value = value + (1.0 if (j - 1) % 2 else -1.0)
                    st[j, f - 1, pl.ds(b * 32 + (xh * 2 + yh) * 8, 8), :] = value

            own = [[cells(ref, b, xh, yh) for yh in (0, 1)] for xh in (0, 1)]
            for yh in (0, 1):
                xpad[f, yh, 7:8, :] = low[2 * f + yh : 2 * f + yh + 1]
                xpad[f, yh, 24:25, :] = high[2 * f + yh : 2 * f + yh + 1]
                for xh in (0, 1):
                    xpad[f, yh, 8 + 8 * xh : 16 + 8 * xh, :] = own[xh][yh]
            for xh in (0, 1):
                ghost = [table[src[k] + 2 * (f // 2) + xh] for k in range(2, 6)]
                mixed = jnp.where(
                    group < 2,
                    jnp.where(group == 0, ghost[1], ghost[0]),
                    jnp.where(group == 2, ghost[3], ghost[2]),
                )
                up = [pltpu.roll(own[xh][yh], 16, 1) for yh in (0, 1)]
                down = [pltpu.roll(own[xh][yh], LANES - 16, 1) for yh in (0, 1)]
                gy = [pick(mixed, spread_y[f % 2][yh]) for yh in (0, 1)]
                for yh in (0, 1):
                    mine = own[xh][yh]
                    gz = pick(mixed, spread_z[f % 2][yh])
                    put(0, xh, yh, mine)
                    put(1, xh, yh, xpad[f, yh, 7 + 8 * xh : 15 + 8 * xh, :])
                    put(2, xh, yh, xpad[f, yh, 9 + 8 * xh : 17 + 8 * xh, :])
                    put(3, xh, yh, jnp.where(lane < 16, gy[0] if yh == 0 else up[0], up[yh]))
                    put(4, xh, yh, jnp.where(lane >= 112, gy[1] if yh == 1 else down[1], down[yh]))
                    put(5, xh, yh, jnp.where(lane % 16 == 0, gz, pltpu.roll(mine, 1, 1)))
                    put(6, xh, yh, jnp.where(lane % 16 == 15, gz, pltpu.roll(mine, LANES - 1, 1)))
        return carry

    lax.fori_loop(0, BLK, block, 0)


def plane_faces(velo_ref, params, pf):
    lane = lane_ids()
    row = row_ids()
    l = lane % 128
    index = jnp.where(
        l < 48, l % 16, jnp.where(l < 64, l + 64, 16 * (l % 8) + jnp.where(l < 80, 0, 15))
    )
    upper = ((l >= 48) & (l < 64)) | ((l >= 72) & (l < 80)) | ((l >= 88) & (l < 96))
    unroll_x = row * 16 + lane % 16

    def block(b, carry):
        def face(first, second, third):
            for h in (0, 1):
                low = pick(jnp.broadcast_to(first[0][h][0:1], (8, LANES)), unroll_x)
                high = pick(jnp.broadcast_to(first[1][h][7:8], (8, LANES)), unroll_x)
                if second is third:
                    zero, one = second[h]
                else:
                    zero = second[h][0], third[h][0]
                    one = second[h][1], third[h][1]
                if second is third:
                    sides = jnp.where(upper, pick(one, index), pick(zero, index))
                else:
                    sides = jnp.where(
                        l < 64,
                        jnp.where(upper, pick(one[0], index), pick(zero[0], index)),
                        jnp.where(upper, pick(one[1], index), pick(zero[1], index)),
                    )
                yield h, jnp.where(l < 16, low, jnp.where(l < 32, high, sides))

        for comp in range(4):
            value = [
                [params[comp, pl.ds(b * 32 + (xh * 2 + yh) * 8, 8), :] for yh in (0, 1)]
                for xh in (0, 1)
            ]
            for h, packed in face(value, value, value):
                pf[b * 5 + comp, 8 * h : 8 * h + 8, :] = packed
        speed = [
            [[cells(velo_ref.at[axis], b, xh, yh) for yh in (0, 1)] for xh in (0, 1)]
            for axis in range(3)
        ]
        for h, packed in face(*speed):
            pf[b * 5 + 4, 8 * h : 8 * h + 8, :] = packed
        return carry

    lax.fori_loop(0, BLK, block, 0)


def fine_slots(refine_ref, pf, slots):
    lane = lane_ids()

    def slot(s, carry):
        f = refine_ref[s * 2]
        k = refine_ref[s * 2 + 1]
        index = k * 16 + 2 * (lane % 8) + (lane // 8) % 2
        odd = (lane // 16) % 2 == 1
        parts = []
        for comp in (lax.shift_right_logical(k, 1), 3, 4):
            even_rows = pf[f * 5 + comp, pl.ds(0, 8, stride=2), :]
            odd_rows = pf[f * 5 + comp, pl.ds(1, 8, stride=2), :]
            parts.append(jnp.where(odd, pick(odd_rows, index), pick(even_rows, index)))
        slots[s] = jnp.where(lane < 32, parts[0], jnp.where(lane < 64, parts[1], parts[2]))
        return carry

    lax.fori_loop(0, SLOTS, slot, 0, unroll=4)


def fit_kernel(
    tbl_ref, refine_ref, own_ref, r1_ref, r2_ref, r3_ref, r4_ref, r5_ref, frac_ref, cent_ref, velo_ref,
    planes_ref, pf_ref, slots_ref, table, xpad, st, params,
):
    lane = lane_ids()
    for at, ref in enumerate((own_ref, r1_ref, r2_ref, r3_ref, r4_ref, r5_ref)):

        def copy(i, carry, at=at, ref=ref):
            for u in range(6):
                table[at * 48 + i * 6 + u] = ref[i * 6 + u]
            return carry

        lax.fori_loop(0, BLK, copy, 0)

    def swap(i, carry):
        for u in range(2, 6):
            v = own_ref[i * 6 + u]
            odd = (lane // 16) % 2 == 1
            table[288 + i * 6 + u] = jnp.where(
                odd, pltpu.roll(v, 16, 1), pltpu.roll(v, LANES - 16, 1)
            )
        return carry

    lax.fori_loop(0, BLK, swap, 0)
    stencil(tbl_ref, frac_ref, cent_ref, table, xpad, st)

    rows = GROUP * 8

    def fit(i, carry):
        at = pl.ds(pl.multiple_of(i * rows, rows), rows)

        def load(j):
            return tuple(st[j, c, at, :] for c in range(4))

        values = lax.fori_loop(0, PASSES, lambda _, p: one_pass(load, p), start(load))
        for comp in range(4):
            params[comp, at, :] = values[comp]
        return carry

    lax.fori_loop(0, 32 // GROUP, fit, 0)

    def emit(b, carry):
        for comp in range(4):
            for xh in (0, 1):
                for yh in (0, 1):
                    planes_ref[pl.ds(b * 128 + 64 * xh + 4 * yh + comp, 8, stride=8), :] = params[
                        comp, pl.ds(b * 32 + (xh * 2 + yh) * 8, 8), :
                    ]
        return carry

    lax.fori_loop(0, BLK, emit, 0)
    plane_faces(velo_ref, params, pf_ref)
    fine_slots(refine_ref, pf_ref, slots_ref)


def moment_kernel(
    meta_ref, pf_ref, s0_ref, s1_ref, s2_ref, s3_ref, s4_ref, s5_ref, out_ref, slots, todo
):
    lane = lane_ids()
    row = row_ids()
    out_ref[...] = jnp.zeros_like(out_ref)
    for at, ref in enumerate((s0_ref, s1_ref, s2_ref, s3_ref, s4_ref, s5_ref)):
        for u in range(SLOTS):
            slots[at * SLOTS + u] = ref[u]
    total = PARTS * SLOTS

    def collect(i, n):
        todo[n] = i
        return n + meta_ref[i]

    count = lax.fori_loop(0, total, collect, 0, unroll=8)
    for extra in range(4):
        todo[count + extra] = 0
    quarter = lane // 32
    first_off = (((lane // 16) % 2).astype(jnp.float32) - 0.5) * 0.5
    second_off = (((lane // 8) % 2).astype(jnp.float32) - 0.5) * 0.5

    def group(g, carry):
        fine = [None] * 3
        coarse = [None] * 5
        sign = None
        weight = None
        where = []

        def merge(old, new, q):
            return new if old is None else jnp.where(quarter == q, new, old)

        for q in range(4):
            at = 4 * g + q
            i = todo[at]
            c = meta_ref[total + i]
            k = meta_ref[2 * total + i]
            quad = meta_ref[3 * total + i]
            axis = lax.shift_right_logical(k, 1)
            qa = lax.shift_right_logical(quad, 1)
            qb = quad & 1
            source = slots[i]
            for comp in range(3):
                turn = ((q - comp) * 32) % LANES
                moved = source if turn == 0 else pltpu.roll(source, turn, 1)
                fine[comp] = merge(fine[comp], moved, q)
            index = k * 16 + qb * 8 + lane % 8
            which = (axis, jnp.where(axis == 0, 1, 0), jnp.where(axis == 2, 1, 2), 3, 4)
            for at_comp, comp in enumerate(which):
                value = pf_ref[c * 5 + comp, pl.ds(pl.multiple_of(qa * 8, 8), 8), :]
                coarse[at_comp] = merge(coarse[at_comp], pick(value, index), q)
            s = jnp.where((k & 1) == 1, -1.0, 1.0).astype(jnp.float32)
            sign = merge(sign, jnp.full((8, LANES), s, jnp.float32), q)
            on = jnp.where(at < count, 1.0, 0.0).astype(jnp.float32)
            weight = merge(weight, jnp.full((8, LANES), on, jnp.float32), q)
            where.append((((c * 6 + k) * 2 + qa) * 2, qb))
        an, df, uf = fine
        cn, t1, t2, dc, uc = coarse
        speed = sign * 0.5 * (uf + uc)
        depth = jnp.abs(speed) * TIME_STEP
        outflow = jnp.maximum(speed, 0.0)
        inflow = jnp.minimum(speed, 0.0)
        base = t1 * first_off + t2 * second_off + dc
        volume = 0.0
        moment = 0.0
        for node in NODES:
            fine_phase = an * (sign * (0.5 - node * depth)) + df
            coarse_phase = cn * (-sign * (0.5 - 0.5 * node * depth)) + base
            fine_model = 0.5 * (1.0 + jnp.tanh(fine_phase))
            coarse_model = 0.5 * (1.0 + jnp.tanh(coarse_phase))
            gain = outflow * fine_model
            loss = inflow * coarse_model
            volume = volume + 0.5 * TIME_STEP * (gain + loss)
            moment = moment + 0.5 * TIME_STEP * node * depth * sign * (loss - gain)
        sums = []
        for value in (volume * weight, moment * weight):
            value = value + pltpu.roll(value, LANES - 8, 1)
            sums.append(value + pltpu.roll(value, LANES - 16, 1))
        for q in range(4):
            target, qb = where[q]
            index = 32 * q + lane % 8
            keep = (lane // 16 == row) & ((lane // 8) % 2 == qb)
            rows = [
                jnp.sum(jnp.where(keep, pick(value, index), 0.0), axis=0, keepdims=True)
                for value in sums
            ]
            for m in range(2):
                out_ref[pl.ds(target + m, 1), :] = out_ref[pl.ds(target + m, 1), :] + rows[m]
        return carry

    lax.fori_loop(0, (count + 3) // 4, group, 0)


def partners(n, distance, offset):
    pairs = []
    for i in range(n):
        up = ((i - offset) // distance) % 2 == 0
        j = i + distance if up else i - distance
        pairs.append((i, j if 0 <= j < n else i ^ 1))
    return pairs


def trade(value):
    n = lax.axis_size("sfc")
    inside, near, far = partners(n, 1, 0), partners(n, 2, 0), partners(n, 2, 2)
    far_same = lax.ppermute(value, "sfc", far)
    near_same = lax.ppermute(value, "sfc", near)
    sibling = lax.ppermute(value, "sfc", inside)
    far_other = lax.ppermute(far_same, "sfc", inside)
    near_other = lax.ppermute(near_same, "sfc", inside)
    return [sibling, near_same, far_same, near_other, far_other]


def tiles(field):
    return field.reshape(BLK, 32, LANES).transpose(1, 0, 2).reshape(256, LANES)


def tiles3(field):
    return field.reshape(BLK, 3, 32, LANES).transpose(1, 2, 0, 3).reshape(3, 256, LANES)


def per_device(fraction, centroid, velocity, neighbours, refinement):
    f32 = jnp.float32
    i32 = jnp.int32
    me = lax.axis_index("sfc").astype(i32)
    frac, cent, velo = tiles(fraction), tiles3(centroid), tiles3(velocity)
    out = functools.partial(jax.ShapeDtypeStruct, dtype=f32)
    limit = pltpu.CompilerParams(vmem_limit_bytes=48 << 20)

    faces = pl.pallas_call(
        pack_kernel,
        out_shape=out((49, 8, LANES)),
        in_specs=[pl.BlockSpec(memory_space=pltpu.HBM)] * 3,
        out_specs=VMEM_SPEC,
        scratch_shapes=[
            pltpu.VMEM((4, 256, LANES), f32),
            pltpu.VMEM((4, SLOTS), i32),
            pltpu.SemaphoreType.DMA((5,)),
        ],
        compiler_params=limit,
        name="pack",
    )(*(pltpu.with_memory_space_constraint(v, pltpu.HBM) for v in (frac, cent, refinement.T)))
    got = trade(faces)

    device = neighbours // BLK
    step = device // 2 - me // 2
    near_step = 1 - 2 * ((me // 2) % 2)
    part = jnp.where(
        step == 0,
        jnp.where(device == me, 0, 1),
        jnp.where(step == near_step, 2, 3) + jnp.where(device % 2 == me % 2, 0, 2),
    )
    direction = jnp.arange(6, dtype=i32)[None, :]
    block = jnp.arange(BLK, dtype=i32)[:, None]
    inside = part * BLK + neighbours % BLK
    x_row = jnp.where(neighbours >= 0, inside * 6 + 1 - direction, block * 6 + direction)
    yz_row = jnp.where(neighbours >= 0, inside, 48 + block) * 6 + 2
    rows = jnp.where(direction < 2, x_row, yz_row)
    rows = jnp.clip(rows, 0, 333).reshape(48)

    fine_local = jnp.clip(refinement[:, 0] - me * BLK, 0, BLK - 1)
    fine_side = jnp.clip(refinement[:, 1], 0, 5)
    fine_table = jnp.stack([fine_local, fine_side], axis=1).reshape(2 * SLOTS)

    planes, plane_face, slots = pl.pallas_call(
        fit_kernel,
        out_shape=(out((1024, LANES)), out((BLK * 5, 16, LANES)), out((SLOTS, 8, LANES))),
        in_specs=[SMEM_SPEC] * 2 + [VMEM_SPEC] * 9,
        out_specs=(VMEM_SPEC,) * 3,
        scratch_shapes=[
            pltpu.VMEM((336, 8, LANES), f32),
            pltpu.VMEM((4, 2, 32, LANES), f32),
            pltpu.VMEM((7, 4, 256, LANES), f32),
            pltpu.VMEM((4, 256, LANES), f32),
        ],
        compiler_params=limit,
        name="fit",
    )(rows, fine_table, faces, *got, frac, cent, velo)

    got_slots = trade(slots)
    count = lax.axis_size("sfc")
    twice = (me // 2 == 0) | (me // 2 == count // 2 - 1)
    tables = jnp.stack(
        [refinement.T] + [v[48, 0:4, 0:SLOTS].astype(i32) for v in got], axis=1
    )
    part_ids = jnp.arange(PARTS, dtype=i32)[:, None]
    fresh = jnp.logical_not(twice & ((part_ids == 3) | (part_ids == 5)))
    mine = (tables[0] >= 0) & (tables[2] // BLK == me) & fresh
    side = jnp.clip(tables[1], 0, 5)
    meta = jnp.stack(
        [
            mine.astype(i32),
            jnp.clip(tables[2], 0, None) % BLK,
            side + 1 - 2 * (side % 2),
            jnp.clip(tables[3], 0, 3),
        ]
    ).reshape(4 * PARTS * SLOTS)

    reflux = pl.pallas_call(
        moment_kernel,
        out_shape=out((BLK * 6 * 4, LANES)),
        in_specs=[SMEM_SPEC] + [VMEM_SPEC] * 7,
        out_specs=VMEM_SPEC,
        scratch_shapes=[
            pltpu.VMEM((PARTS * SLOTS, 8, LANES), f32),
            pltpu.SMEM((PARTS * SLOTS + 8,), i32),
        ],
        compiler_params=limit,
        name="moments",
    )(meta, plane_face, slots, *got_slots)

    planes = planes.reshape(BLK, 32, 4, LANES).transpose(0, 2, 1, 3).reshape(BLK, 4, 4096)
    reflux = reflux.reshape(BLK, 6, 2, 2, LANES).transpose(0, 1, 3, 2, 4).reshape(BLK, 6, 2, 256)
    return planes, reflux


def solution(mesh):
    return jax.shard_map(
        per_device,
        mesh=mesh,
        in_specs=(
            P("sfc", None),
            P("sfc", None, None),
            P("sfc", None, None),
            P("sfc", None),
            P("sfc", None),
        ),
        out_specs=(P("sfc", None, None), P("sfc", None, None, None)),
        check_vma=False,
    )
```

```python
import functools

import jax
import jax.numpy as jnp
from jax import lax
from jax.experimental import pallas as pl
from jax.experimental.pallas import tpu as pltpu
from jax.sharding import PartitionSpec as P

BLK = 8
SLOTS = 16
PARTS = 6
TODO = 112
PASSES = 6
LANES = 128
NODES = (0.5 - 3.0**0.5 / 6.0, 0.5 + 3.0**0.5 / 6.0)
TIME_STEP = 0.25
DAMPING = 0.1
VMEM_SPEC = pl.BlockSpec(memory_space=pltpu.VMEM)
SMEM_SPEC = pl.BlockSpec(memory_space=pltpu.SMEM)


def lane_ids():
    return lax.broadcasted_iota(jnp.int32, (8, LANES), 1)


def row_ids():
    return lax.broadcasted_iota(jnp.int32, (8, LANES), 0)


def pick(values, index):
    return jnp.take_along_axis(values, index, axis=1, mode="promise_in_bounds")


def cells(ref, b, xh, yh):
    return ref[pl.ds(xh * 128 + yh * 8 + b, 8, stride=16), :]


def side_index(lane):
    l = lane % 64
    index = jnp.where(l < 16, l, jnp.where(l < 32, l + 96, 16 * (l % 8) + jnp.where(l < 48, 0, 15)))
    upper = ((l >= 16) & (l < 32)) | ((l >= 40) & (l < 48)) | (l >= 56)
    return index, upper


def pack_kernel(
    frac_hbm, cent_hbm, refine_hbm, near_hbm, out_ref, field, refine_ref, near_ref, sems
):
    copies = [
        pltpu.make_async_copy(frac_hbm if f == 0 else cent_hbm.at[f - 1], field.at[f], sems.at[f])
        for f in range(4)
    ]
    copies.append(pltpu.make_async_copy(refine_hbm, refine_ref, sems.at[4]))
    copies.append(pltpu.make_async_copy(near_hbm, near_ref, sems.at[5]))
    for copy in copies:
        copy.start()
    lane = lane_ids()
    index, upper = side_index(lane)
    out_ref[48] = jnp.zeros((8, LANES), jnp.float32)
    for copy in copies:
        copy.wait()
    out_ref[48, 0:4, 0:SLOTS] = refine_ref[...].astype(jnp.float32)

    def block(b, carry):
        for xh in (0, 1):
            sides = []
            for f in range(4):
                half = [cells(field.at[f], b, xh, yh) for yh in (0, 1)]
                for yh in (0, 1):
                    row = half[yh][0:1] if xh == 0 else half[yh][7:8]
                    out_ref[b * 6 + xh, 2 * f + yh : 2 * f + yh + 1, :] = row
                sides.append(jnp.where(upper, pick(half[1], index), pick(half[0], index)))
            for fp in (0, 1):
                out_ref[b * 6 + 2 + 2 * fp + xh] = jnp.where(lane < 64, sides[2 * fp], sides[2 * fp + 1])
        return carry

    lax.fori_loop(0, BLK, block, 0)


def solve(h, g):
    a, b, c = h[0][0], h[0][1], h[1][1]
    ra = 1.0 / (a * c - b * b)
    ia, ib, ic = c * ra, b * ra, a * ra
    p, q, r, s = h[0][2], h[0][3], h[1][2], h[1][3]
    wp, wq = ia * p - ib * r, ia * q - ib * s
    wr, ws = ic * r - ib * p, ic * s - ib * q
    sa = h[2][2] - p * wp - r * wr
    sb = h[2][3] - p * wq - r * ws
    sc = h[3][3] - q * wq - s * ws
    z0, z1 = ia * g[0] - ib * g[1], ic * g[1] - ib * g[0]
    y0 = g[2] - p * z0 - r * z1
    y1 = g[3] - q * z0 - s * z1
    rs = 1.0 / (sa * sc - sb * sb)
    x2 = (sc * y0 - sb * y1) * rs
    x3 = (sa * y1 - sb * y0) * rs
    return z0 - wp * x2 - wq * x3, z1 - wr * x2 - ws * x3, x2, x3


def one_pass(load, params):
    a, b, c, d = params
    h = [[None] * 4 for _ in range(4)]
    g = [None] * 4

    def add(total, value):
        return value if total is None else total + value

    for j in range(7):
        px, py, pz, q = load(j)
        t = jnp.tanh(a * px + b * py + c * pz + d)
        s = 1.0 - t * t
        w = s * s
        r = s * (t + q)
        wx, wy, wz = w * px, w * py, w * pz
        h[0][0] = add(h[0][0], wx * px)
        h[0][1] = add(h[0][1], wx * py)
        h[0][2] = add(h[0][2], wx * pz)
        h[0][3] = add(h[0][3], wx)
        h[1][1] = add(h[1][1], wy * py)
        h[1][2] = add(h[1][2], wy * pz)
        h[1][3] = add(h[1][3], wy)
        h[2][2] = add(h[2][2], wz * pz)
        h[2][3] = add(h[2][3], wz)
        h[3][3] = add(h[3][3], w)
        g[0] = add(g[0], r * px)
        g[1] = add(g[1], r * py)
        g[2] = add(g[2], r * pz)
        g[3] = add(g[3], r)
    for i in range(4):
        h[i][i] = h[i][i] + 4.0 * DAMPING
    step = solve(h, g)
    return tuple(p - u for p, u in zip(params, step))


def start(load):
    f = [0.5 - 0.5 * load(j)[3] for j in range(7)]
    cx, cy, cz, _ = load(0)
    a, b, c = (2.0 * (f[2 * k + 2] - f[2 * k + 1]) for k in range(3))
    d = 2.0 * (2.0 * f[0] - 1.0) - a * cx - b * cy - c * cz
    return a, b, c, d


def held_as(f, j, value):
    if f == 0:
        return 1.0 - 2.0 * value
    if j > 0 and (j - 1) // 2 == f - 1:
        return value + (1.0 if (j - 1) % 2 else -1.0)
    return value


def own_points(field, xpad, st):
    lane = lane_ids()

    def block(b, carry):
        for f in range(4):

            def put(j, xh, yh, value):
                at = pl.ds(b * 32 + yh * 16 + xh * 8, 8)
                st[j, (f + 3) % 4, at, :] = held_as(f, j, value)

            own = [[cells(field.at[f], b, xh, yh) for yh in (0, 1)] for xh in (0, 1)]
            for yh in (0, 1):
                for xh in (0, 1):
                    xpad[f, yh, 8 + 8 * xh : 16 + 8 * xh, :] = own[xh][yh]
            for xh in (0, 1):
                up = [pltpu.roll(own[xh][yh], 16, 1) for yh in (0, 1)]
                down = [pltpu.roll(own[xh][yh], LANES - 16, 1) for yh in (0, 1)]
                for yh in (0, 1):
                    mine = own[xh][yh]
                    put(0, xh, yh, mine)
                    put(1, xh, yh, xpad[f, yh, 7 + 8 * xh : 15 + 8 * xh, :])
                    put(2, xh, yh, xpad[f, yh, 9 + 8 * xh : 17 + 8 * xh, :])
                    put(3, xh, yh, up[0] if yh == 0 else jnp.where(lane < 16, up[0], up[1]))
                    put(4, xh, yh, down[1] if yh == 1 else jnp.where(lane >= 112, down[1], down[0]))
                    put(5, xh, yh, pltpu.roll(mine, 1, 1))
                    put(6, xh, yh, pltpu.roll(mine, LANES - 1, 1))
        return carry

    xpad[...] = jnp.zeros_like(xpad)
    lax.fori_loop(0, BLK, block, 0)


def patch(b, tbl_ref, table, st):
    lane = lane_ids()
    group = (lane % 64) // 16
    src = [tbl_ref[b * 6 + k] for k in range(6)]
    low, high = table[src[0]], table[src[1]]

    def put(j, f, at, mask, value):
        c = (f + 3) % 4
        st[j, c, at, :] = jnp.where(mask, held_as(f, j, value), st[j, c, at, :])

    for f in range(4):
        c = (f + 3) % 4
        for yh in (0, 1):
            row = b * 32 + yh * 16
            st[1, c, row : row + 1, :] = held_as(f, 1, low[2 * f + yh : 2 * f + yh + 1])
            st[2, c, row + 15 : row + 16, :] = held_as(f, 2, high[2 * f + yh : 2 * f + yh + 1])
    for fp in (0, 1):
        for xh in (0, 1):
            ghost = [table[src[k] + 2 * fp + xh] for k in range(2, 6)]
            mixed = jnp.where(
                group < 2,
                jnp.where(group == 0, ghost[1], ghost[0]),
                jnp.where(group == 2, ghost[3], ghost[2]),
            )
            for fh in (0, 1):
                f = 2 * fp + fh
                for yh in (0, 1):
                    row = b * 32 + yh * 16 + xh * 8
                    at = slice(row, row + 8)
                    index = fh * 64 + jnp.where(lane % 16 == 15, 32, 48) + yh * 8 + lane // 16
                    value = pick(mixed, index)
                    put(5, f, at, lane % 16 == 0, value)
                    put(6, f, at, lane % 16 == 15, value)
                    value = pick(mixed, fh * 64 + (16 if yh == 0 else 0) + lane % 16)
                    if yh == 0:
                        put(3, f, at, lane < 16, value)
                    else:
                        put(4, f, at, lane >= 112, value)


def face_index(lane):
    index = jnp.where(
        lane < 48,
        lane % 16,
        jnp.where(lane < 64, lane + 64, 16 * (lane % 8) + jnp.where(lane < 80, 0, 15)),
    )
    upper = (
        ((lane >= 48) & (lane < 64)) | ((lane >= 72) & (lane < 80)) | ((lane >= 88) & (lane < 96))
    )
    return index, upper


def x_faces(lane, row, first, h):
    unroll_x = row * 16 + lane % 16
    low = pick(jnp.broadcast_to(first[0][h][0:1], (8, LANES)), unroll_x)
    high = pick(jnp.broadcast_to(first[1][h][7:8], (8, LANES)), unroll_x)
    return low, high


def prepare_kernel(field, velo_ref, points_hbm, out_ref, xpad, st, sem):
    own_points(field, xpad, st)
    keep = pltpu.make_async_copy(st, points_hbm, sem)
    keep.start()
    lane, row = lane_ids(), row_ids()
    index, upper = face_index(lane)

    def block(b, carry):
        x, y, z = (
            [[cells(velo_ref.at[axis], b, xh, yh) for yh in (0, 1)] for xh in (0, 1)]
            for axis in range(3)
        )
        for h in (0, 1):
            low, high = x_faces(lane, row, x, h)
            y_sides = jnp.where(upper, pick(y[h][1], index), pick(y[h][0], index))
            z_sides = jnp.where(upper, pick(z[h][1], index), pick(z[h][0], index))
            sides = jnp.where(lane < 64, y_sides, z_sides)
            out_ref[b, 8 * h : 8 * h + 8, :] = jnp.where(
                lane < 16, low, jnp.where(lane < 32, high, sides)
            )
        return carry

    lax.fori_loop(0, BLK, block, 0, unroll=2)
    keep.wait()


def plane_faces(params, pf, count, first):
    lane, row = lane_ids(), row_ids()
    index, upper = face_index(lane)

    def block(b, carry):
        for comp in range(4):
            value = [
                [params[comp, pl.ds(b * 32 + yh * 16 + xh * 8, 8), :] for yh in (0, 1)]
                for xh in (0, 1)
            ]
            for h in (0, 1):
                low, high = x_faces(lane, row, value, h)
                sides = jnp.where(upper, pick(value[h][1], index), pick(value[h][0], index))
                pf[(first + b) * 4 + comp, 8 * h : 8 * h + 8, :] = jnp.where(
                    lane < 16, low, jnp.where(lane < 32, high, sides)
                )
        return carry

    lax.fori_loop(0, count, block, 0, unroll=2)


def fine_slots(refine_ref, params, speed_ref, slots_ref):
    lane, row = lane_ids(), row_ids()
    isub = (lane // 16) % 2
    odd = isub == 1
    second = 2 * (lane % 8) + (lane // 8) % 2
    x_source = 16 * ((2 * row + isub) % 8) + second

    def tile(g, carry):
        total = [None] * 3
        for q in range(4):
            f = refine_ref[2 * (4 * g + q)]
            k = refine_ref[2 * (4 * g + q) + 1]
            axis = lax.shift_right_logical(k, 1)
            side = k & 1
            y_source = side * 112 + second
            z_source = 16 * (second % 8) + 15 * side
            is_x = jnp.full((8, LANES), axis, jnp.int32) == 0
            is_y = jnp.full((8, LANES), axis, jnp.int32) == 1
            upper = second >= 8
            got = []
            for comp in (axis, 3):
                at = f * 32
                ref = params.at[comp]
                line = at + side * 15
                x_value = pick(
                    jnp.where(
                        row < 4,
                        jnp.broadcast_to(ref[pl.ds(line, 1), :], (8, LANES)),
                        jnp.broadcast_to(ref[pl.ds(line + 16, 1), :], (8, LANES)),
                    ),
                    x_source,
                )
                part = [
                    [ref[pl.ds(at + 16 * yh + sub, 8, stride=2), :] for yh in (0, 1)]
                    for sub in (0, 1)
                ]
                high_side = jnp.full((8, LANES), side, jnp.int32) == 1
                y_part = [pick(jnp.where(high_side, p[1], p[0]), y_source) for p in part]
                z_part = [jnp.where(upper, pick(p[1], z_source), pick(p[0], z_source)) for p in part]
                got.append(
                    jnp.where(
                        is_x,
                        x_value,
                        jnp.where(
                            is_y,
                            jnp.where(odd, y_part[1], y_part[0]),
                            jnp.where(odd, z_part[1], z_part[0]),
                        ),
                    )
                )
            index = k * 16 + second
            got.append(
                jnp.where(
                    odd,
                    pick(speed_ref[f, pl.ds(1, 8, stride=2), :], index),
                    pick(speed_ref[f, pl.ds(0, 8, stride=2), :], index),
                )
            )
            for comp in range(3):
                old = total[comp]
                total[comp] = got[comp] if q == 0 else jnp.where(lane // 32 == q, got[comp], old)
        for comp in range(3):
            slots_ref[4 * comp + g] = total[comp]
        return carry

    lax.fori_loop(0, SLOTS // 4, tile, 0)


def fit_kernel(
    tbl_ref, refine_ref, own_ref, r1_ref, r2_ref, r3_ref, r4_ref, r5_ref, points_hbm, speed_ref,
    params, slots_ref, st, table, sems,
):
    fetches = [
        pltpu.make_async_copy(
            points_hbm.at[:, :, pl.ds(b * 32, 32), :], st.at[:, :, pl.ds(b * 32, 32), :], sems.at[b]
        )
        for b in range(BLK)
    ]
    for fetch in fetches:
        fetch.start()
    lane = lane_ids()
    for at, ref in enumerate((own_ref, r1_ref, r2_ref, r3_ref, r4_ref, r5_ref)):

        def copy(i, carry, at=at, ref=ref):
            for u in range(12):
                table[at * 48 + i * 12 + u] = ref[i * 12 + u]
            return carry

        lax.fori_loop(0, 4, copy, 0)

    def swap(i, carry):
        for u in range(2, 6):
            v = own_ref[i * 6 + u]
            odd = (lane // 16) % 2 == 1
            table[288 + i * 6 + u] = jnp.where(
                odd, pltpu.roll(v, 16, 1), pltpu.roll(v, LANES - 16, 1)
            )
        return carry

    lax.fori_loop(0, BLK, swap, 0, unroll=2)
    for b in range(BLK):
        fetches[b].wait()
        patch(b, tbl_ref, table, st)
        at = slice(b * 32, b * 32 + 32)

        def load(j, at=at):
            return tuple(st[j, c, at, :] for c in range(4))

        values = lax.fori_loop(0, PASSES, lambda _, p, load=load: one_pass(load, p), start(load))
        for comp in range(4):
            params[comp, at, :] = values[comp]
    fine_slots(refine_ref, params, speed_ref, slots_ref)


def emit_kernel(meta_ref, params, planes_hbm, pf_ref, todo_ref, buffer, sem):
    def emit(b, carry):
        for comp in range(4):
            for xh in (0, 1):
                for yh in (0, 1):
                    buffer[pl.ds(b * 128 + 64 * xh + 4 * yh + comp, 8, stride=8), :] = params[
                        comp, pl.ds(b * 32 + yh * 16 + xh * 8, 8), :
                    ]
        return carry

    lax.fori_loop(0, BLK, emit, 0)
    copy = pltpu.make_async_copy(buffer, planes_hbm, sem)
    copy.start()
    plane_faces(params, pf_ref, BLK, 0)

    def collect(i, n):
        todo_ref[n] = i
        return n + meta_ref[i]

    count = lax.fori_loop(0, PARTS * SLOTS, collect, 0, unroll=8)
    for extra in range(4):
        todo_ref[count + extra] = 0
    todo_ref[TODO - 1] = count
    copy.wait()


def moment_kernel(
    meta_ref, todo, pf_ref, speed_ref, s0_ref, s1_ref, s2_ref, s3_ref, s4_ref, s5_ref, out_ref, slots
):
    lane = lane_ids()
    row = row_ids()
    out_ref[...] = jnp.zeros_like(out_ref)
    for at, ref in enumerate((s0_ref, s1_ref, s2_ref, s3_ref, s4_ref, s5_ref)):
        for u in range(12):
            slots[at * 12 + u] = ref[u]
    total = PARTS * SLOTS

    count = todo[TODO - 1]
    quarter = lane // 32
    first_off = (((lane // 16) % 2).astype(jnp.float32) - 0.5) * 0.5
    second_off = (((lane // 8) % 2).astype(jnp.float32) - 0.5) * 0.5

    def group(g, carry):
        fine = [None] * 3
        coarse = [None] * 5
        sign = None
        weight = None
        where = []

        def merge(old, new, q):
            return new if old is None else jnp.where(quarter == q, new, old)

        for q in range(4):
            at = 4 * g + q
            i = todo[at]
            c = meta_ref[total + i]
            k = meta_ref[2 * total + i]
            quad = meta_ref[3 * total + i]
            axis = lax.shift_right_logical(k, 1)
            qa = lax.shift_right_logical(quad, 1)
            qb = quad & 1
            held = lax.shift_right_logical(i, 4) * 12 + (lax.shift_right_logical(i, 2) & 3)
            turn = (i & 3) * 32 + lane % 32
            for comp in range(3):
                fine[comp] = merge(fine[comp], pick(slots[held + 4 * comp], turn), q)
            index = k * 16 + qb * 8 + lane % 8
            which = (axis, jnp.where(axis == 0, 1, 0), jnp.where(axis == 2, 1, 2), 3, 4)
            for at_comp, comp in enumerate(which):
                rows_at = pl.ds(pl.multiple_of(qa * 8, 8), 8)
                value = speed_ref[c, rows_at, :] if at_comp == 4 else pf_ref[c * 4 + comp, rows_at, :]
                coarse[at_comp] = merge(coarse[at_comp], pick(value, index), q)
            s = jnp.where((k & 1) == 1, -1.0, 1.0).astype(jnp.float32)
            sign = merge(sign, jnp.full((8, LANES), s, jnp.float32), q)
            on = jnp.where(at < count, 1.0, 0.0).astype(jnp.float32)
            weight = merge(weight, jnp.full((8, LANES), on, jnp.float32), q)
            where.append((((c * 6 + k) * 2 + qa) * 2, qb))
        an, df, uf = fine
        cn, t1, t2, dc, uc = coarse
        speed = sign * 0.5 * (uf + uc)
        depth = jnp.abs(speed) * TIME_STEP
        outflow = jnp.maximum(speed, 0.0)
        inflow = jnp.minimum(speed, 0.0)
        base = t1 * first_off + t2 * second_off + dc
        volume = 0.0
        moment = 0.0
        for node in NODES:
            fine_phase = an * (sign * (0.5 - node * depth)) + df
            coarse_phase = cn * (-sign * (0.5 - 0.5 * node * depth)) + base
            fine_model = 0.5 * (1.0 + jnp.tanh(fine_phase))
            coarse_model = 0.5 * (1.0 + jnp.tanh(coarse_phase))
            gain = outflow * fine_model
            loss = inflow * coarse_model
            volume = volume + 0.5 * TIME_STEP * (gain + loss)
            moment = moment + 0.5 * TIME_STEP * node * depth * sign * (loss - gain)
        sums = []
        for value in (volume * weight, moment * weight):
            value = value + pltpu.roll(value, LANES - 8, 1)
            sums.append(value + pltpu.roll(value, LANES - 16, 1))
        for q in range(4):
            target, qb = where[q]
            index = 32 * q + lane % 8
            keep = (lane // 16 == row) & ((lane // 8) % 2 == qb)
            rows = [
                jnp.sum(jnp.where(keep, pick(value, index), 0.0), axis=0, keepdims=True)
                for value in sums
            ]
            for m in range(2):
                out_ref[pl.ds(target + m, 1), :] = out_ref[pl.ds(target + m, 1), :] + rows[m]
        return carry

    lax.fori_loop(0, (count + 3) // 4, group, 0)


def partners(n, distance, offset):
    pairs = []
    for i in range(n):
        up = ((i - offset) // distance) % 2 == 0
        j = i + distance if up else i - distance
        pairs.append((i, j if 0 <= j < n else i ^ 1))
    return pairs


def trade(value):
    n = lax.axis_size("sfc")
    far = lax.ppermute(value, "sfc", partners(n, 2, 2))
    near = lax.ppermute(value, "sfc", partners(n, 2, 0))
    return [lax.ppermute(value, "sfc", partners(n, 1, 0)), near, far]


def relay(values):
    inside = partners(lax.axis_size("sfc"), 1, 0)
    return [lax.ppermute(value, "sfc", inside) for value in values]


def tiles(field):
    return field.reshape(BLK, 32, LANES).transpose(1, 0, 2).reshape(256, LANES)


def tiles3(field):
    return field.reshape(BLK, 3, 32, LANES).transpose(1, 2, 0, 3).reshape(3, 256, LANES)


def lasting(microseconds):
    return pl.CostEstimate(flops=0, transcendentals=0, bytes_accessed=microseconds * 3_500_000)


def per_device(fraction, centroid, velocity, neighbours, refinement):
    f32 = jnp.float32
    i32 = jnp.int32
    me = lax.axis_index("sfc").astype(i32)
    frac, cent, velo = tiles(fraction), tiles3(centroid), tiles3(velocity)
    out = functools.partial(jax.ShapeDtypeStruct, dtype=f32)
    limit = pltpu.CompilerParams(vmem_limit_bytes=12 << 20)

    hbm = pl.BlockSpec(memory_space=pltpu.HBM)
    faces, field, fine_rows, neighbours = pl.pallas_call(
        pack_kernel,
        out_shape=(
            out((49, 8, LANES)),
            out((4, 256, LANES)),
            jax.ShapeDtypeStruct((4, SLOTS), i32),
            jax.ShapeDtypeStruct((BLK, 6), i32),
        ),
        in_specs=[hbm] * 4,
        out_specs=(VMEM_SPEC,) * 4,
        scratch_shapes=[pltpu.SemaphoreType.DMA((6,))],
        compiler_params=limit,
        name="pack",
    )(*(pltpu.with_memory_space_constraint(v, pltpu.HBM) for v in (frac, cent, refinement.T, neighbours)))
    got = trade(faces)
    got = got + relay(got[1:])

    device = neighbours // BLK
    step = device // 2 - me // 2
    near_step = 1 - 2 * ((me // 2) % 2)
    part = jnp.where(
        step == 0,
        jnp.where(device == me, 0, 1),
        jnp.where(step == near_step, 2, 3) + jnp.where(device % 2 == me % 2, 0, 2),
    )
    direction = jnp.arange(6, dtype=i32)[None, :]
    block = jnp.arange(BLK, dtype=i32)[:, None]
    inside = part * BLK + neighbours % BLK
    x_row = jnp.where(neighbours >= 0, inside * 6 + 1 - direction, block * 6 + direction)
    yz_row = jnp.where(neighbours >= 0, inside, 48 + block) * 6 + 2
    rows = jnp.where(direction < 2, x_row, yz_row)
    rows = jnp.clip(rows, 0, 333).reshape(48)

    fine_local = jnp.clip(fine_rows[0] - me * BLK, 0, BLK - 1)
    fine_side = jnp.clip(fine_rows[1], 0, 5)
    fine_table = jnp.stack([fine_local, fine_side], axis=1).reshape(2 * SLOTS)

    points, speed = pl.pallas_call(
        prepare_kernel,
        out_shape=(pltpu.HBM((7, 4, 256, LANES), f32), out((BLK, 16, LANES))),
        in_specs=[VMEM_SPEC] * 2,
        out_specs=(hbm, VMEM_SPEC),
        scratch_shapes=[
            pltpu.VMEM((4, 2, 32, LANES), f32),
            pltpu.VMEM((7, 4, 256, LANES), f32),
            pltpu.SemaphoreType.DMA,
        ],
        compiler_params=limit,
        cost_estimate=lasting(4),
        name="prepare",
    )(field, velo)
    points = pltpu.with_memory_space_constraint(points, pltpu.HBM)
    params, slots = pl.pallas_call(
        fit_kernel,
        out_shape=(out((4, 256, LANES)), out((12, 8, LANES))),
        in_specs=[SMEM_SPEC] * 2 + [VMEM_SPEC] * 6 + [hbm, VMEM_SPEC],
        out_specs=(VMEM_SPEC,) * 2,
        scratch_shapes=[
            pltpu.VMEM((7, 4, 256, LANES), f32),
            pltpu.VMEM((336, 8, LANES), f32),
            pltpu.SemaphoreType.DMA((BLK,)),
        ],
        compiler_params=limit,
        cost_estimate=lasting(12),
        name="fit",
    )(rows, fine_table, faces, *got, points, speed)
    got_slots = trade(slots)

    count = lax.axis_size("sfc")
    twice = (me // 2 == 0) | (me // 2 == count // 2 - 1)
    tables = jnp.stack(
        [fine_rows] + [v[48, 0:4, 0:SLOTS].astype(i32) for v in got], axis=1
    )
    part_ids = jnp.arange(PARTS, dtype=i32)[:, None]
    fresh = jnp.logical_not(twice & ((part_ids == 3) | (part_ids == 5)))
    mine = (tables[0] >= 0) & (tables[2] // BLK == me) & fresh
    side = jnp.clip(tables[1], 0, 5)
    meta = jnp.stack(
        [
            mine.astype(i32),
            jnp.clip(tables[2], 0, None) % BLK,
            side + 1 - 2 * (side % 2),
            jnp.clip(tables[3], 0, 3),
        ]
    ).reshape(4 * PARTS * SLOTS)

    planes, plane_face, todo = pl.pallas_call(
        emit_kernel,
        out_shape=(
            out((1024, LANES)),
            out((BLK * 4, 16, LANES)),
            jax.ShapeDtypeStruct((TODO,), i32),
        ),
        in_specs=[SMEM_SPEC, VMEM_SPEC],
        out_specs=(hbm, VMEM_SPEC, SMEM_SPEC),
        scratch_shapes=[pltpu.VMEM((1024, LANES), f32), pltpu.SemaphoreType.DMA],
        compiler_params=limit,
        cost_estimate=lasting(2),
        name="emit",
    )(meta, params)
    plane_face, near, far = lax.optimization_barrier((plane_face, *got_slots[1:]))
    got_slots = [got_slots[0], near, far] + relay([near, far])

    reflux = pl.pallas_call(
        moment_kernel,
        out_shape=out((BLK * 6 * 4, LANES)),
        in_specs=[SMEM_SPEC] * 2 + [VMEM_SPEC] * 8,
        out_specs=VMEM_SPEC,
        scratch_shapes=[pltpu.VMEM((PARTS * 12, 8, LANES), f32)],
        compiler_params=limit,
        name="moments",
    )(meta, todo, plane_face, speed, slots, *got_slots)

    planes = planes.reshape(BLK, 32, 4, LANES).transpose(0, 2, 1, 3).reshape(BLK, 4, 4096)
    reflux = reflux.reshape(BLK, 6, 2, 2, LANES).transpose(0, 1, 3, 2, 4).reshape(BLK, 6, 2, 256)
    return planes, reflux


def solution(mesh):
    return jax.shard_map(
        per_device,
        mesh=mesh,
        in_specs=(
            P("sfc", None),
            P("sfc", None, None),
            P("sfc", None, None),
            P("sfc", None),
            P("sfc", None),
        ),
        out_specs=(P("sfc", None, None), P("sfc", None, None, None)),
        check_vma=False,
    )
```

```python
import functools

import jax
import jax.numpy as jnp
from jax import lax
from jax.experimental import pallas as pl
from jax.experimental.pallas import tpu as pltpu
from jax.sharding import PartitionSpec as P

BLK = 8
SLOTS = 16
PARTS = 6
TODO = 112
PASSES = 6
LANES = 128
NODES = (0.5 - 3.0**0.5 / 6.0, 0.5 + 3.0**0.5 / 6.0)
TIME_STEP = 0.25
DAMPING = 0.1
VMEM_SPEC = pl.BlockSpec(memory_space=pltpu.VMEM)
SMEM_SPEC = pl.BlockSpec(memory_space=pltpu.SMEM)


def lane_ids():
    return lax.broadcasted_iota(jnp.int32, (8, LANES), 1)


def row_ids():
    return lax.broadcasted_iota(jnp.int32, (8, LANES), 0)


def pick(values, index):
    return jnp.take_along_axis(values, index, axis=1, mode="promise_in_bounds")


def cells(ref, b, xh, yh):
    return ref[pl.ds(xh * 128 + yh * 8 + b, 8, stride=16), :]


def side_index(lane):
    l = lane % 64
    index = jnp.where(l < 16, l, jnp.where(l < 32, l + 96, 16 * (l % 8) + jnp.where(l < 48, 0, 15)))
    upper = ((l >= 16) & (l < 32)) | ((l >= 40) & (l < 48)) | (l >= 56)
    return index, upper


def pack_kernel(
    frac_hbm, cent_hbm, refine_hbm, near_hbm, out_ref, field, refine_ref, near_ref, sems
):
    copies = [
        pltpu.make_async_copy(frac_hbm if f == 0 else cent_hbm.at[f - 1], field.at[f], sems.at[f])
        for f in range(4)
    ]
    copies.append(pltpu.make_async_copy(refine_hbm, refine_ref, sems.at[4]))
    copies.append(pltpu.make_async_copy(near_hbm, near_ref, sems.at[5]))
    for copy in copies:
        copy.start()
    lane = lane_ids()
    index, upper = side_index(lane)
    out_ref[48] = jnp.zeros((8, LANES), jnp.float32)
    for fp in (0, 1):

        def block(b, carry, fp=fp):
            for xh in (0, 1):
                sides = []
                for f in (2 * fp, 2 * fp + 1):
                    half = [cells(field.at[f], b, xh, yh) for yh in (0, 1)]
                    for yh in (0, 1):
                        row = half[yh][0:1] if xh == 0 else half[yh][7:8]
                        out_ref[b * 6 + xh, 2 * f + yh : 2 * f + yh + 1, :] = row
                    sides.append(jnp.where(upper, pick(half[1], index), pick(half[0], index)))
                out_ref[b * 6 + 2 + 2 * fp + xh] = jnp.where(lane < 64, sides[0], sides[1])
            return carry

        copies[2 * fp].wait()
        copies[2 * fp + 1].wait()
        lax.fori_loop(0, BLK, block, 0, unroll=4)
    for copy in copies[4:]:
        copy.wait()
    out_ref[48, 0:4, 0:SLOTS] = refine_ref[...].astype(jnp.float32)


def solve(h, g):
    a, b, c = h[0][0], h[0][1], h[1][1]
    ra = 1.0 / (a * c - b * b)
    ia, ib, ic = c * ra, b * ra, a * ra
    p, q, r, s = h[0][2], h[0][3], h[1][2], h[1][3]
    wp, wq = ia * p - ib * r, ia * q - ib * s
    wr, ws = ic * r - ib * p, ic * s - ib * q
    sa = h[2][2] - p * wp - r * wr
    sb = h[2][3] - p * wq - r * ws
    sc = h[3][3] - q * wq - s * ws
    z0, z1 = ia * g[0] - ib * g[1], ic * g[1] - ib * g[0]
    y0 = g[2] - p * z0 - r * z1
    y1 = g[3] - q * z0 - s * z1
    rs = 1.0 / (sa * sc - sb * sb)
    x2 = (sc * y0 - sb * y1) * rs
    x3 = (sa * y1 - sb * y0) * rs
    return z0 - wp * x2 - wq * x3, z1 - wr * x2 - ws * x3, x2, x3


def one_pass(load, params):
    a, b, c, d = params
    h = [[None] * 4 for _ in range(4)]
    g = [None] * 4

    def add(total, value):
        return value if total is None else total + value

    for j in range(7):
        px, py, pz, q = load(j)
        t = jnp.tanh(a * px + b * py + c * pz + d)
        s = 1.0 - t * t
        w = s * s
        r = s * (t + q)
        wx, wy, wz = w * px, w * py, w * pz
        h[0][0] = add(h[0][0], wx * px)
        h[0][1] = add(h[0][1], wx * py)
        h[0][2] = add(h[0][2], wx * pz)
        h[0][3] = add(h[0][3], wx)
        h[1][1] = add(h[1][1], wy * py)
        h[1][2] = add(h[1][2], wy * pz)
        h[1][3] = add(h[1][3], wy)
        h[2][2] = add(h[2][2], wz * pz)
        h[2][3] = add(h[2][3], wz)
        h[3][3] = add(h[3][3], w)
        g[0] = add(g[0], r * px)
        g[1] = add(g[1], r * py)
        g[2] = add(g[2], r * pz)
        g[3] = add(g[3], r)
    for i in range(4):
        h[i][i] = h[i][i] + 4.0 * DAMPING
    step = solve(h, g)
    return tuple(p - u for p, u in zip(params, step))


def start(load):
    f = [0.5 - 0.5 * load(j)[3] for j in range(7)]
    cx, cy, cz, _ = load(0)
    a, b, c = (2.0 * (f[2 * k + 2] - f[2 * k + 1]) for k in range(3))
    d = 2.0 * (2.0 * f[0] - 1.0) - a * cx - b * cy - c * cz
    return a, b, c, d


def held_as(f, j, value):
    if f == 0:
        return 1.0 - 2.0 * value
    if j > 0 and (j - 1) // 2 == f - 1:
        return value + (1.0 if (j - 1) % 2 else -1.0)
    return value


def own_points(field, xpad, st):
    lane = lane_ids()

    def block(b, carry):
        for f in range(4):

            def put(j, xh, yh, value):
                at = pl.ds(b * 32 + yh * 16 + xh * 8, 8)
                st[j, (f + 3) % 4, at, :] = held_as(f, j, value)

            own = [[cells(field.at[f], b, xh, yh) for yh in (0, 1)] for xh in (0, 1)]
            for yh in (0, 1):
                for xh in (0, 1):
                    xpad[f, yh, 8 + 8 * xh : 16 + 8 * xh, :] = own[xh][yh]
            for xh in (0, 1):
                up = [pltpu.roll(own[xh][yh], 16, 1) for yh in (0, 1)]
                down = [pltpu.roll(own[xh][yh], LANES - 16, 1) for yh in (0, 1)]
                for yh in (0, 1):
                    mine = own[xh][yh]
                    put(0, xh, yh, mine)
                    put(1, xh, yh, xpad[f, yh, 7 + 8 * xh : 15 + 8 * xh, :])
                    put(2, xh, yh, xpad[f, yh, 9 + 8 * xh : 17 + 8 * xh, :])
                    put(3, xh, yh, up[0] if yh == 0 else jnp.where(lane < 16, up[0], up[1]))
                    put(4, xh, yh, down[1] if yh == 1 else jnp.where(lane >= 112, down[1], down[0]))
                    put(5, xh, yh, pltpu.roll(mine, 1, 1))
                    put(6, xh, yh, pltpu.roll(mine, LANES - 1, 1))
        return carry

    xpad[...] = jnp.zeros_like(xpad)
    lax.fori_loop(0, BLK, block, 0)


def patch(b, tbl_ref, table, st):
    lane = lane_ids()
    group = (lane % 64) // 16
    src = [tbl_ref[b * 6 + k] for k in range(6)]
    low, high = table[src[0]], table[src[1]]

    def put(j, f, at, mask, value):
        c = (f + 3) % 4
        st[j, c, at, :] = jnp.where(mask, held_as(f, j, value), st[j, c, at, :])

    for f in range(4):
        c = (f + 3) % 4
        for yh in (0, 1):
            row = b * 32 + yh * 16
            st[1, c, row : row + 1, :] = held_as(f, 1, low[2 * f + yh : 2 * f + yh + 1])
            st[2, c, row + 15 : row + 16, :] = held_as(f, 2, high[2 * f + yh : 2 * f + yh + 1])
    for fp in (0, 1):
        for xh in (0, 1):
            ghost = [table[src[k] + 2 * fp + xh] for k in range(2, 6)]
            mixed = jnp.where(
                group < 2,
                jnp.where(group == 0, ghost[1], ghost[0]),
                jnp.where(group == 2, ghost[3], ghost[2]),
            )
            for fh in (0, 1):
                f = 2 * fp + fh
                for yh in (0, 1):
                    row = b * 32 + yh * 16 + xh * 8
                    at = slice(row, row + 8)
                    index = fh * 64 + jnp.where(lane % 16 == 15, 32, 48) + yh * 8 + lane // 16
                    value = pick(mixed, index)
                    put(5, f, at, lane % 16 == 0, value)
                    put(6, f, at, lane % 16 == 15, value)
                    value = pick(mixed, fh * 64 + (16 if yh == 0 else 0) + lane % 16)
                    if yh == 0:
                        put(3, f, at, lane < 16, value)
                    else:
                        put(4, f, at, lane >= 112, value)


def face_index(lane):
    index = jnp.where(
        lane < 48,
        lane % 16,
        jnp.where(lane < 64, lane + 64, 16 * (lane % 8) + jnp.where(lane < 80, 0, 15)),
    )
    upper = (
        ((lane >= 48) & (lane < 64)) | ((lane >= 72) & (lane < 80)) | ((lane >= 88) & (lane < 96))
    )
    return index, upper


def x_faces(lane, row, first, h):
    unroll_x = row * 16 + lane % 16
    low = pick(jnp.broadcast_to(first[0][h][0:1], (8, LANES)), unroll_x)
    high = pick(jnp.broadcast_to(first[1][h][7:8], (8, LANES)), unroll_x)
    return low, high


def prepare_kernel(field, velo_ref, points_hbm, out_ref, xpad, st, sem):
    own_points(field, xpad, st)
    keep = pltpu.make_async_copy(st, points_hbm, sem)
    keep.start()
    lane, row = lane_ids(), row_ids()
    index, upper = face_index(lane)

    def block(b, carry):
        x, y, z = (
            [[cells(velo_ref.at[axis], b, xh, yh) for yh in (0, 1)] for xh in (0, 1)]
            for axis in range(3)
        )
        for h in (0, 1):
            low, high = x_faces(lane, row, x, h)
            y_sides = jnp.where(upper, pick(y[h][1], index), pick(y[h][0], index))
            z_sides = jnp.where(upper, pick(z[h][1], index), pick(z[h][0], index))
            sides = jnp.where(lane < 64, y_sides, z_sides)
            out_ref[b, 8 * h : 8 * h + 8, :] = jnp.where(
                lane < 16, low, jnp.where(lane < 32, high, sides)
            )
        return carry

    lax.fori_loop(0, BLK, block, 0, unroll=2)
    keep.wait()


def plane_faces(params, pf, count, first):
    lane, row = lane_ids(), row_ids()
    index, upper = face_index(lane)

    def block(b, carry):
        for comp in range(4):
            value = [
                [params[comp, pl.ds(b * 32 + yh * 16 + xh * 8, 8), :] for yh in (0, 1)]
                for xh in (0, 1)
            ]
            for h in (0, 1):
                low, high = x_faces(lane, row, value, h)
                sides = jnp.where(upper, pick(value[h][1], index), pick(value[h][0], index))
                pf[(first + b) * 4 + comp, 8 * h : 8 * h + 8, :] = jnp.where(
                    lane < 16, low, jnp.where(lane < 32, high, sides)
                )
        return carry

    lax.fori_loop(0, count, block, 0, unroll=2)


def fine_slots(refine_ref, params, speed_ref, slots_ref):
    lane, row = lane_ids(), row_ids()
    isub = (lane // 16) % 2
    odd = isub == 1
    second = 2 * (lane % 8) + (lane // 8) % 2
    x_source = 16 * ((2 * row + isub) % 8) + second

    def tile(g, carry):
        total = [None] * 3
        for q in range(4):
            f = refine_ref[2 * (4 * g + q)]
            k = refine_ref[2 * (4 * g + q) + 1]
            axis = lax.shift_right_logical(k, 1)
            side = k & 1
            y_source = side * 112 + second
            z_source = 16 * (second % 8) + 15 * side
            is_x = jnp.full((8, LANES), axis, jnp.int32) == 0
            is_y = jnp.full((8, LANES), axis, jnp.int32) == 1
            upper = second >= 8
            got = []
            for comp in (axis, 3):
                at = f * 32
                ref = params.at[comp]
                line = at + side * 15
                x_value = pick(
                    jnp.where(
                        row < 4,
                        jnp.broadcast_to(ref[pl.ds(line, 1), :], (8, LANES)),
                        jnp.broadcast_to(ref[pl.ds(line + 16, 1), :], (8, LANES)),
                    ),
                    x_source,
                )
                part = [
                    [ref[pl.ds(at + 16 * yh + sub, 8, stride=2), :] for yh in (0, 1)]
                    for sub in (0, 1)
                ]
                high_side = jnp.full((8, LANES), side, jnp.int32) == 1
                y_part = [pick(jnp.where(high_side, p[1], p[0]), y_source) for p in part]
                z_part = [jnp.where(upper, pick(p[1], z_source), pick(p[0], z_source)) for p in part]
                got.append(
                    jnp.where(
                        is_x,
                        x_value,
                        jnp.where(
                            is_y,
                            jnp.where(odd, y_part[1], y_part[0]),
                            jnp.where(odd, z_part[1], z_part[0]),
                        ),
                    )
                )
            index = k * 16 + second
            got.append(
                jnp.where(
                    odd,
                    pick(speed_ref[f, pl.ds(1, 8, stride=2), :], index),
                    pick(speed_ref[f, pl.ds(0, 8, stride=2), :], index),
                )
            )
            for comp in range(3):
                old = total[comp]
                total[comp] = got[comp] if q == 0 else jnp.where(lane // 32 == q, got[comp], old)
        for comp in range(3):
            slots_ref[4 * comp + g] = total[comp]
        return carry

    lax.fori_loop(0, SLOTS // 4, tile, 0, unroll=2)


def fit_kernel(
    tbl_ref, refine_ref, own_ref, r1_ref, r2_ref, r3_ref, r4_ref, r5_ref, points_hbm, speed_ref,
    params, slots_ref, st, table, sems,
):
    fetches = [
        pltpu.make_async_copy(
            points_hbm.at[:, :, pl.ds(b * 32, 32), :], st.at[:, :, pl.ds(b * 32, 32), :], sems.at[b]
        )
        for b in range(BLK)
    ]
    fetches[0].start()
    fetches[1].start()
    lane = lane_ids()
    for at, ref in enumerate((own_ref, r1_ref, r2_ref, r3_ref, r4_ref, r5_ref)):

        def copy(i, carry, at=at, ref=ref):
            for u in range(12):
                table[at * 48 + i * 12 + u] = ref[i * 12 + u]
            return carry

        lax.fori_loop(0, 4, copy, 0)

    def swap(i, carry):
        for u in range(2, 6):
            v = own_ref[i * 6 + u]
            odd = (lane // 16) % 2 == 1
            table[288 + i * 6 + u] = jnp.where(
                odd, pltpu.roll(v, 16, 1), pltpu.roll(v, LANES - 16, 1)
            )
        return carry

    lax.fori_loop(0, BLK, swap, 0, unroll=2)
    for b in range(BLK):
        fetches[b].wait()
        if b + 2 < BLK:
            fetches[b + 2].start()
        patch(b, tbl_ref, table, st)
        at = slice(b * 32, b * 32 + 32)

        def load(j, at=at):
            return tuple(st[j, c, at, :] for c in range(4))

        values = lax.fori_loop(0, PASSES, lambda _, p, load=load: one_pass(load, p), start(load), unroll=6)
        for comp in range(4):
            params[comp, at, :] = values[comp]
    fine_slots(refine_ref, params, speed_ref, slots_ref)


def emit_kernel(meta_ref, params, planes_hbm, pf_ref, todo_ref, buffer, sem):
    def emit(b, carry):
        for comp in range(4):
            for xh in (0, 1):
                for yh in (0, 1):
                    buffer[pl.ds(b * 128 + 64 * xh + 4 * yh + comp, 8, stride=8), :] = params[
                        comp, pl.ds(b * 32 + yh * 16 + xh * 8, 8), :
                    ]
        return carry

    lax.fori_loop(0, BLK, emit, 0)
    copy = pltpu.make_async_copy(buffer, planes_hbm, sem)
    copy.start()
    plane_faces(params, pf_ref, BLK, 0)

    def collect(i, n):
        todo_ref[n] = meta_ref[PARTS * SLOTS + i]
        return n + meta_ref[i]

    count = lax.fori_loop(0, PARTS * SLOTS, collect, 0, unroll=8)
    for extra in range(4):
        todo_ref[count + extra] = 0
    todo_ref[TODO - 1] = count
    copy.wait()


def moment_kernel(
    todo, pf_ref, speed_ref, s0_ref, s1_ref, s2_ref, s3_ref, s4_ref, s5_ref, out_ref, slots
):
    lane = lane_ids()
    row = row_ids()
    out_ref[...] = jnp.zeros_like(out_ref)
    for at, ref in enumerate((s0_ref, s1_ref, s2_ref, s3_ref, s4_ref, s5_ref)):
        for u in range(12):
            slots[at * 12 + u] = ref[u]

    count = todo[TODO - 1]
    quarter = lane // 32
    first_off = (((lane // 16) % 2).astype(jnp.float32) - 0.5) * 0.5
    second_off = (((lane // 8) % 2).astype(jnp.float32) - 0.5) * 0.5

    def group(g, carry):
        fine = [None] * 3
        coarse = [None] * 5
        sign = None
        weight = None
        where = []

        def merge(old, new, q):
            return new if old is None else jnp.where(quarter == q, new, old)

        for q in range(4):
            at = 4 * g + q
            entry = todo[at]
            i = entry & 127
            c = lax.shift_right_logical(entry, 7) & 7
            k = lax.shift_right_logical(entry, 10) & 7
            quad = lax.shift_right_logical(entry, 13)
            axis = lax.shift_right_logical(k, 1)
            qa = lax.shift_right_logical(quad, 1)
            qb = quad & 1
            held = lax.shift_right_logical(i, 4) * 12 + (lax.shift_right_logical(i, 2) & 3)
            turn = (i & 3) * 32 + lane % 32
            for comp in range(3):
                fine[comp] = merge(fine[comp], pick(slots[held + 4 * comp], turn), q)
            index = k * 16 + qb * 8 + lane % 8
            which = (axis, jnp.where(axis == 0, 1, 0), jnp.where(axis == 2, 1, 2), 3, 4)
            for at_comp, comp in enumerate(which):
                rows_at = pl.ds(pl.multiple_of(qa * 8, 8), 8)
                value = speed_ref[c, rows_at, :] if at_comp == 4 else pf_ref[c * 4 + comp, rows_at, :]
                coarse[at_comp] = merge(coarse[at_comp], pick(value, index), q)
            s = jnp.where((k & 1) == 1, -1.0, 1.0).astype(jnp.float32)
            sign = merge(sign, jnp.full((8, LANES), s, jnp.float32), q)
            on = jnp.where(at < count, 1.0, 0.0).astype(jnp.float32)
            weight = merge(weight, jnp.full((8, LANES), on, jnp.float32), q)
            where.append((((c * 6 + k) * 2 + qa) * 2, qb))
        an, df, uf = fine
        cn, t1, t2, dc, uc = coarse
        speed = sign * 0.5 * (uf + uc)
        depth = jnp.abs(speed) * TIME_STEP
        outflow = jnp.maximum(speed, 0.0)
        inflow = jnp.minimum(speed, 0.0)
        base = t1 * first_off + t2 * second_off + dc
        volume = 0.0
        moment = 0.0
        for node in NODES:
            fine_phase = an * (sign * (0.5 - node * depth)) + df
            coarse_phase = cn * (-sign * (0.5 - 0.5 * node * depth)) + base
            fine_model = 0.5 * (1.0 + jnp.tanh(fine_phase))
            coarse_model = 0.5 * (1.0 + jnp.tanh(coarse_phase))
            gain = outflow * fine_model
            loss = inflow * coarse_model
            volume = volume + 0.5 * TIME_STEP * (gain + loss)
            moment = moment + 0.5 * TIME_STEP * node * depth * sign * (loss - gain)
        sums = []
        for value in (volume * weight, moment * weight):
            value = value + pltpu.roll(value, LANES - 8, 1)
            sums.append(value + pltpu.roll(value, LANES - 16, 1))
        for q in range(4):
            target, qb = where[q]
            index = 32 * q + lane % 8
            keep = (lane // 16 == row) & ((lane // 8) % 2 == qb)
            rows = [
                jnp.sum(jnp.where(keep, pick(value, index), 0.0), axis=0, keepdims=True)
                for value in sums
            ]
            for m in range(2):
                out_ref[pl.ds(target + m, 1), :] = out_ref[pl.ds(target + m, 1), :] + rows[m]
        return carry

    lax.fori_loop(0, (count + 3) // 4, group, 0)


def partners(n, distance, offset):
    pairs = []
    for i in range(n):
        up = ((i - offset) // distance) % 2 == 0
        j = i + distance if up else i - distance
        pairs.append((i, j if 0 <= j < n else i ^ 1))
    return pairs


def trade(value):
    n = lax.axis_size("sfc")
    far = lax.ppermute(value, "sfc", partners(n, 2, 2))
    near = lax.ppermute(value, "sfc", partners(n, 2, 0))
    return [lax.ppermute(value, "sfc", partners(n, 1, 0)), near, far]


def relay(values):
    inside = partners(lax.axis_size("sfc"), 1, 0)
    return [lax.ppermute(value, "sfc", inside) for value in values]


def tiles(field):
    return field.reshape(BLK, 32, LANES).transpose(1, 0, 2).reshape(256, LANES)


def tiles3(field):
    return field.reshape(BLK, 3, 32, LANES).transpose(1, 2, 0, 3).reshape(3, 256, LANES)


def lasting(microseconds):
    return pl.CostEstimate(flops=0, transcendentals=0, bytes_accessed=microseconds * 3_500_000)


def per_device(fraction, centroid, velocity, neighbours, refinement):
    f32 = jnp.float32
    i32 = jnp.int32
    me = lax.axis_index("sfc").astype(i32)
    frac, cent, velo = tiles(fraction), tiles3(centroid), tiles3(velocity)
    out = functools.partial(jax.ShapeDtypeStruct, dtype=f32)
    limit = pltpu.CompilerParams(vmem_limit_bytes=12 << 20)

    hbm = pl.BlockSpec(memory_space=pltpu.HBM)
    faces, field, fine_rows, neighbours = pl.pallas_call(
        pack_kernel,
        out_shape=(
            out((49, 8, LANES)),
            out((4, 256, LANES)),
            jax.ShapeDtypeStruct((4, SLOTS), i32),
            jax.ShapeDtypeStruct((BLK, 6), i32),
        ),
        in_specs=[hbm] * 4,
        out_specs=(VMEM_SPEC,) * 4,
        scratch_shapes=[pltpu.SemaphoreType.DMA((6,))],
        compiler_params=limit,
        name="pack",
    )(*(pltpu.with_memory_space_constraint(v, pltpu.HBM) for v in (frac, cent, refinement.T, neighbours)))
    got = trade(faces)
    got = got + relay(got[1:])

    device = neighbours // BLK
    step = device // 2 - me // 2
    near_step = 1 - 2 * ((me // 2) % 2)
    part = jnp.where(
        step == 0,
        jnp.where(device == me, 0, 1),
        jnp.where(step == near_step, 2, 3) + jnp.where(device % 2 == me % 2, 0, 2),
    )
    direction = jnp.arange(6, dtype=i32)[None, :]
    block = jnp.arange(BLK, dtype=i32)[:, None]
    inside = part * BLK + neighbours % BLK
    x_row = jnp.where(neighbours >= 0, inside * 6 + 1 - direction, block * 6 + direction)
    yz_row = jnp.where(neighbours >= 0, inside, 48 + block) * 6 + 2
    rows = jnp.where(direction < 2, x_row, yz_row)
    rows = jnp.clip(rows, 0, 333).reshape(48)

    fine_local = jnp.clip(fine_rows[0] - me * BLK, 0, BLK - 1)
    fine_side = jnp.clip(fine_rows[1], 0, 5)
    fine_table = jnp.stack([fine_local, fine_side], axis=1).reshape(2 * SLOTS)

    points, speed = pl.pallas_call(
        prepare_kernel,
        out_shape=(pltpu.HBM((7, 4, 256, LANES), f32), out((BLK, 16, LANES))),
        in_specs=[VMEM_SPEC] * 2,
        out_specs=(hbm, VMEM_SPEC),
        scratch_shapes=[
            pltpu.VMEM((4, 2, 32, LANES), f32),
            pltpu.VMEM((7, 4, 256, LANES), f32),
            pltpu.SemaphoreType.DMA,
        ],
        compiler_params=limit,
        cost_estimate=lasting(4),
        name="prepare",
    )(field, velo)
    points = pltpu.with_memory_space_constraint(points, pltpu.HBM)
    params, slots = pl.pallas_call(
        fit_kernel,
        out_shape=(out((4, 256, LANES)), out((12, 8, LANES))),
        in_specs=[SMEM_SPEC] * 2 + [VMEM_SPEC] * 6 + [hbm, VMEM_SPEC],
        out_specs=(VMEM_SPEC,) * 2,
        scratch_shapes=[
            pltpu.VMEM((7, 4, 256, LANES), f32),
            pltpu.VMEM((336, 8, LANES), f32),
            pltpu.SemaphoreType.DMA((BLK,)),
        ],
        compiler_params=limit,
        cost_estimate=lasting(12),
        name="fit",
    )(rows, fine_table, faces, *got, points, speed)
    got_slots = trade(slots)

    count = lax.axis_size("sfc")
    twice = (me // 2 == 0) | (me // 2 == count // 2 - 1)
    tables = jnp.stack(
        [fine_rows] + [v[48, 0:4, 0:SLOTS].astype(i32) for v in got], axis=1
    )
    part_ids = jnp.arange(PARTS, dtype=i32)[:, None]
    fresh = jnp.logical_not(twice & ((part_ids == 3) | (part_ids == 5)))
    mine = (tables[0] >= 0) & (tables[2] // BLK == me) & fresh
    side = jnp.clip(tables[1], 0, 5)
    slot_ids = jnp.arange(PARTS * SLOTS, dtype=i32).reshape(PARTS, SLOTS)
    entry = (
        slot_ids
        + 128 * (jnp.clip(tables[2], 0, None) % BLK)
        + 1024 * (side + 1 - 2 * (side % 2))
        + 8192 * jnp.clip(tables[3], 0, 3)
    )
    meta = jnp.stack([mine.astype(i32), entry]).reshape(2 * PARTS * SLOTS)

    planes, plane_face, todo = pl.pallas_call(
        emit_kernel,
        out_shape=(
            out((1024, LANES)),
            out((BLK * 4, 16, LANES)),
            jax.ShapeDtypeStruct((TODO,), i32),
        ),
        in_specs=[SMEM_SPEC, VMEM_SPEC],
        out_specs=(hbm, VMEM_SPEC, SMEM_SPEC),
        scratch_shapes=[pltpu.VMEM((1024, LANES), f32), pltpu.SemaphoreType.DMA],
        compiler_params=limit,
        cost_estimate=lasting(2),
        name="emit",
    )(meta, params)
    plane_face, near, far = lax.optimization_barrier((plane_face, *got_slots[1:]))
    got_slots = [got_slots[0], near, far] + relay([near, far])

    reflux = pl.pallas_call(
        moment_kernel,
        out_shape=out((BLK * 6 * 4, LANES)),
        in_specs=[SMEM_SPEC] + [VMEM_SPEC] * 8,
        out_specs=VMEM_SPEC,
        scratch_shapes=[pltpu.VMEM((PARTS * 12, 8, LANES), f32)],
        compiler_params=limit,
        name="moments",
    )(todo, plane_face, speed, slots, *got_slots)

    planes = planes.reshape(BLK, 32, 4, LANES).transpose(0, 2, 1, 3).reshape(BLK, 4, 4096)
    reflux = reflux.reshape(BLK, 6, 2, 2, LANES).transpose(0, 1, 3, 2, 4).reshape(BLK, 6, 2, 256)
    return planes, reflux


def solution(mesh):
    return jax.shard_map(
        per_device,
        mesh=mesh,
        in_specs=(
            P("sfc", None),
            P("sfc", None, None),
            P("sfc", None, None),
            P("sfc", None),
            P("sfc", None),
        ),
        out_specs=(P("sfc", None, None), P("sfc", None, None, None)),
        check_vma=False,
    )
```

```python
import functools

import jax
import jax.numpy as jnp
from jax import lax
from jax.experimental import pallas as pl
from jax.experimental.pallas import tpu as pltpu
from jax.sharding import PartitionSpec as P

BLK = 8
SLOTS = 16
PARTS = 6
TODO = 112
EARLY = 4
PASSES = 6
LANES = 128
NODES = (0.5 - 3.0**0.5 / 6.0, 0.5 + 3.0**0.5 / 6.0)
TIME_STEP = 0.25
DAMPING = 0.1
VMEM_SPEC = pl.BlockSpec(memory_space=pltpu.VMEM)
SMEM_SPEC = pl.BlockSpec(memory_space=pltpu.SMEM)


def lane_ids():
    return lax.broadcasted_iota(jnp.int32, (8, LANES), 1)


def row_ids():
    return lax.broadcasted_iota(jnp.int32, (8, LANES), 0)


def pick(values, index):
    return jnp.take_along_axis(values, index, axis=1, mode="promise_in_bounds")


def cells(ref, b, xh, yh):
    return ref[pl.ds(xh * 128 + yh * 8 + b, 8, stride=16), :]


def side_index(lane):
    l = lane % 64
    index = jnp.where(l < 16, l, jnp.where(l < 32, l + 96, 16 * (l % 8) + jnp.where(l < 48, 0, 15)))
    upper = ((l >= 16) & (l < 32)) | ((l >= 40) & (l < 48)) | (l >= 56)
    return index, upper


def pack_kernel(
    frac_hbm, cent_hbm, refine_hbm, near_hbm, out_ref, field, refine_ref, near_ref, sems
):
    copies = [
        pltpu.make_async_copy(frac_hbm if f == 0 else cent_hbm.at[f - 1], field.at[f], sems.at[f])
        for f in range(4)
    ]
    copies.append(pltpu.make_async_copy(refine_hbm, refine_ref, sems.at[4]))
    copies.append(pltpu.make_async_copy(near_hbm, near_ref, sems.at[5]))
    for copy in copies:
        copy.start()
    lane = lane_ids()
    index, upper = side_index(lane)
    out_ref[48] = jnp.zeros((8, LANES), jnp.float32)
    for fp in (0, 1):

        def block(b, carry, fp=fp):
            for xh in (0, 1):
                sides = []
                for f in (2 * fp, 2 * fp + 1):
                    half = [cells(field.at[f], b, xh, yh) for yh in (0, 1)]
                    for yh in (0, 1):
                        row = half[yh][0:1] if xh == 0 else half[yh][7:8]
                        out_ref[b * 6 + xh, 2 * f + yh : 2 * f + yh + 1, :] = row
                    sides.append(jnp.where(upper, pick(half[1], index), pick(half[0], index)))
                out_ref[b * 6 + 2 + 2 * fp + xh] = jnp.where(lane < 64, sides[0], sides[1])
            return carry

        copies[2 * fp].wait()
        copies[2 * fp + 1].wait()
        lax.fori_loop(0, BLK, block, 0, unroll=4)
    for copy in copies[4:]:
        copy.wait()
    out_ref[48, 0:4, 0:SLOTS] = refine_ref[...].astype(jnp.float32)


def solve(h, g):
    a, b, c = h[0][0], h[0][1], h[1][1]
    ra = 1.0 / (a * c - b * b)
    ia, ib, ic = c * ra, b * ra, a * ra
    p, q, r, s = h[0][2], h[0][3], h[1][2], h[1][3]
    wp, wq = ia * p - ib * r, ia * q - ib * s
    wr, ws = ic * r - ib * p, ic * s - ib * q
    sa = h[2][2] - p * wp - r * wr
    sb = h[2][3] - p * wq - r * ws
    sc = h[3][3] - q * wq - s * ws
    z0, z1 = ia * g[0] - ib * g[1], ic * g[1] - ib * g[0]
    y0 = g[2] - p * z0 - r * z1
    y1 = g[3] - q * z0 - s * z1
    rs = 1.0 / (sa * sc - sb * sb)
    x2 = (sc * y0 - sb * y1) * rs
    x3 = (sa * y1 - sb * y0) * rs
    return z0 - wp * x2 - wq * x3, z1 - wr * x2 - ws * x3, x2, x3


def one_pass(load, params):
    a, b, c, d = params
    h = [[None] * 4 for _ in range(4)]
    g = [None] * 4

    def add(total, value):
        return value if total is None else total + value

    for j in range(7):
        px, py, pz, q = load(j)
        t = jnp.tanh(a * px + b * py + c * pz + d)
        s = 1.0 - t * t
        w = s * s
        r = s * (t + q)
        wx, wy, wz = w * px, w * py, w * pz
        h[0][0] = add(h[0][0], wx * px)
        h[0][1] = add(h[0][1], wx * py)
        h[0][2] = add(h[0][2], wx * pz)
        h[0][3] = add(h[0][3], wx)
        h[1][1] = add(h[1][1], wy * py)
        h[1][2] = add(h[1][2], wy * pz)
        h[1][3] = add(h[1][3], wy)
        h[2][2] = add(h[2][2], wz * pz)
        h[2][3] = add(h[2][3], wz)
        h[3][3] = add(h[3][3], w)
        g[0] = add(g[0], r * px)
        g[1] = add(g[1], r * py)
        g[2] = add(g[2], r * pz)
        g[3] = add(g[3], r)
    for i in range(4):
        h[i][i] = h[i][i] + 4.0 * DAMPING
    step = solve(h, g)
    return tuple(p - u for p, u in zip(params, step))


def start(load):
    f = [0.5 - 0.5 * load(j)[3] for j in range(7)]
    cx, cy, cz, _ = load(0)
    a, b, c = (2.0 * (f[2 * k + 2] - f[2 * k + 1]) for k in range(3))
    d = 2.0 * (2.0 * f[0] - 1.0) - a * cx - b * cy - c * cz
    return a, b, c, d


def held_as(f, j, value):
    if f == 0:
        return 1.0 - 2.0 * value
    if j > 0 and (j - 1) // 2 == f - 1:
        return value + (1.0 if (j - 1) % 2 else -1.0)
    return value


def own_points(field, xpad, st):
    lane = lane_ids()

    def block(b, carry):
        for f in range(4):

            def put(j, xh, yh, value):
                at = pl.ds(b * 32 + yh * 16 + xh * 8, 8)
                st[j, (f + 3) % 4, at, :] = held_as(f, j, value)

            own = [[cells(field.at[f], b, xh, yh) for yh in (0, 1)] for xh in (0, 1)]
            for yh in (0, 1):
                for xh in (0, 1):
                    xpad[f, yh, 8 + 8 * xh : 16 + 8 * xh, :] = own[xh][yh]
            for xh in (0, 1):
                up = [pltpu.roll(own[xh][yh], 16, 1) for yh in (0, 1)]
                down = [pltpu.roll(own[xh][yh], LANES - 16, 1) for yh in (0, 1)]
                for yh in (0, 1):
                    mine = own[xh][yh]
                    put(0, xh, yh, mine)
                    put(1, xh, yh, xpad[f, yh, 7 + 8 * xh : 15 + 8 * xh, :])
                    put(2, xh, yh, xpad[f, yh, 9 + 8 * xh : 17 + 8 * xh, :])
                    put(3, xh, yh, up[0] if yh == 0 else jnp.where(lane < 16, up[0], up[1]))
                    put(4, xh, yh, down[1] if yh == 1 else jnp.where(lane >= 112, down[1], down[0]))
                    put(5, xh, yh, pltpu.roll(mine, 1, 1))
                    put(6, xh, yh, pltpu.roll(mine, LANES - 1, 1))
        return carry

    xpad[...] = jnp.zeros_like(xpad)
    lax.fori_loop(0, BLK, block, 0)


def patch(b, tbl_ref, table, st):
    lane = lane_ids()
    group = (lane % 64) // 16
    src = [tbl_ref[b * 6 + k] for k in range(6)]
    low, high = table[src[0]], table[src[1]]

    def put(j, f, at, mask, value):
        c = (f + 3) % 4
        st[j, c, at, :] = jnp.where(mask, held_as(f, j, value), st[j, c, at, :])

    for f in range(4):
        c = (f + 3) % 4
        for yh in (0, 1):
            row = b * 32 + yh * 16
            st[1, c, row : row + 1, :] = held_as(f, 1, low[2 * f + yh : 2 * f + yh + 1])
            st[2, c, row + 15 : row + 16, :] = held_as(f, 2, high[2 * f + yh : 2 * f + yh + 1])
    for fp in (0, 1):
        for xh in (0, 1):
            ghost = [table[src[k] + 2 * fp + xh] for k in range(2, 6)]
            mixed = jnp.where(
                group < 2,
                jnp.where(group == 0, ghost[1], ghost[0]),
                jnp.where(group == 2, ghost[3], ghost[2]),
            )
            for fh in (0, 1):
                f = 2 * fp + fh
                for yh in (0, 1):
                    row = b * 32 + yh * 16 + xh * 8
                    at = slice(row, row + 8)
                    index = fh * 64 + jnp.where(lane % 16 == 15, 32, 48) + yh * 8 + lane // 16
                    value = pick(mixed, index)
                    put(5, f, at, lane % 16 == 0, value)
                    put(6, f, at, lane % 16 == 15, value)
                    value = pick(mixed, fh * 64 + (16 if yh == 0 else 0) + lane % 16)
                    if yh == 0:
                        put(3, f, at, lane < 16, value)
                    else:
                        put(4, f, at, lane >= 112, value)


def face_index(lane):
    index = jnp.where(
        lane < 48,
        lane % 16,
        jnp.where(lane < 64, lane + 64, 16 * (lane % 8) + jnp.where(lane < 80, 0, 15)),
    )
    upper = (
        ((lane >= 48) & (lane < 64)) | ((lane >= 72) & (lane < 80)) | ((lane >= 88) & (lane < 96))
    )
    return index, upper


def x_faces(lane, row, first, h):
    unroll_x = row * 16 + lane % 16
    low = pick(jnp.broadcast_to(first[0][h][0:1], (8, LANES)), unroll_x)
    high = pick(jnp.broadcast_to(first[1][h][7:8], (8, LANES)), unroll_x)
    return low, high


def prepare_kernel(field, velo_hbm, points_hbm, out_ref, xpad, st, velo_ref, sem, velo_sem):
    fetch = pltpu.make_async_copy(velo_hbm, velo_ref, velo_sem)
    fetch.start()
    own_points(field, xpad, st)
    keep = pltpu.make_async_copy(st, points_hbm, sem)
    keep.start()
    fetch.wait()
    lane, row = lane_ids(), row_ids()
    index, upper = face_index(lane)

    def block(b, carry):
        x, y, z = (
            [[cells(velo_ref.at[axis], b, xh, yh) for yh in (0, 1)] for xh in (0, 1)]
            for axis in range(3)
        )
        for h in (0, 1):
            low, high = x_faces(lane, row, x, h)
            y_sides = jnp.where(upper, pick(y[h][1], index), pick(y[h][0], index))
            z_sides = jnp.where(upper, pick(z[h][1], index), pick(z[h][0], index))
            sides = jnp.where(lane < 64, y_sides, z_sides)
            out_ref[b, 8 * h : 8 * h + 8, :] = jnp.where(
                lane < 16, low, jnp.where(lane < 32, high, sides)
            )
        return carry

    lax.fori_loop(0, BLK, block, 0, unroll=2)
    keep.wait()


def plane_faces(params, pf, count, first):
    lane, row = lane_ids(), row_ids()
    index, upper = face_index(lane)

    def block(b, carry):
        for comp in range(4):
            value = [
                [params[comp, pl.ds(b * 32 + yh * 16 + xh * 8, 8), :] for yh in (0, 1)]
                for xh in (0, 1)
            ]
            for h in (0, 1):
                low, high = x_faces(lane, row, value, h)
                sides = jnp.where(upper, pick(value[h][1], index), pick(value[h][0], index))
                pf[(first + b) * 4 + comp, 8 * h : 8 * h + 8, :] = jnp.where(
                    lane < 16, low, jnp.where(lane < 32, high, sides)
                )
        return carry

    lax.fori_loop(0, count, block, 0, unroll=2)


def fine_slots(refine_ref, params, speed_ref, slots_ref):
    lane, row = lane_ids(), row_ids()
    isub = (lane // 16) % 2
    odd = isub == 1
    second = 2 * (lane % 8) + (lane // 8) % 2
    x_source = 16 * ((2 * row + isub) % 8) + second

    def tile(g, carry):
        total = [None] * 3
        for q in range(4):
            f = refine_ref[2 * (4 * g + q)]
            k = refine_ref[2 * (4 * g + q) + 1]
            axis = lax.shift_right_logical(k, 1)
            side = k & 1
            y_source = side * 112 + second
            z_source = 16 * (second % 8) + 15 * side
            is_x = jnp.full((8, LANES), axis, jnp.int32) == 0
            is_y = jnp.full((8, LANES), axis, jnp.int32) == 1
            upper = second >= 8
            got = []
            for comp in (axis, 3):
                at = f * 32
                ref = params.at[comp]
                line = at + side * 15
                x_value = pick(
                    jnp.where(
                        row < 4,
                        jnp.broadcast_to(ref[pl.ds(line, 1), :], (8, LANES)),
                        jnp.broadcast_to(ref[pl.ds(line + 16, 1), :], (8, LANES)),
                    ),
                    x_source,
                )
                part = [
                    [ref[pl.ds(at + 16 * yh + sub, 8, stride=2), :] for yh in (0, 1)]
                    for sub in (0, 1)
                ]
                high_side = jnp.full((8, LANES), side, jnp.int32) == 1
                y_part = [pick(jnp.where(high_side, p[1], p[0]), y_source) for p in part]
                z_part = [jnp.where(upper, pick(p[1], z_source), pick(p[0], z_source)) for p in part]
                got.append(
                    jnp.where(
                        is_x,
                        x_value,
                        jnp.where(
                            is_y,
                            jnp.where(odd, y_part[1], y_part[0]),
                            jnp.where(odd, z_part[1], z_part[0]),
                        ),
                    )
                )
            index = k * 16 + second
            got.append(
                jnp.where(
                    odd,
                    pick(speed_ref[f, pl.ds(1, 8, stride=2), :], index),
                    pick(speed_ref[f, pl.ds(0, 8, stride=2), :], index),
                )
            )
            for comp in range(3):
                old = total[comp]
                total[comp] = got[comp] if q == 0 else jnp.where(lane // 32 == q, got[comp], old)
        for comp in range(3):
            slots_ref[4 * comp + g] = total[comp]
        return carry

    lax.fori_loop(0, SLOTS // 4, tile, 0, unroll=2)


def fit_kernel(
    tbl_ref, refine_ref, own_ref, r1_ref, r2_ref, r3_ref, r4_ref, r5_ref, points_hbm, speed_ref,
    params, slots_ref, st, table, sems,
):
    fetches = [
        pltpu.make_async_copy(
            points_hbm.at[:, :, pl.ds(b * 32, 32), :], st.at[:, :, pl.ds(b * 32, 32), :], sems.at[b]
        )
        for b in range(BLK)
    ]
    fetches[0].start()
    fetches[1].start()
    lane = lane_ids()
    for at, ref in enumerate((own_ref, r1_ref, r2_ref, r3_ref, r4_ref, r5_ref)):

        def copy(i, carry, at=at, ref=ref):
            for u in range(12):
                table[at * 48 + i * 12 + u] = ref[i * 12 + u]
            return carry

        lax.fori_loop(0, 4, copy, 0)

    def swap(i, carry):
        for u in range(2, 6):
            v = own_ref[i * 6 + u]
            odd = (lane // 16) % 2 == 1
            table[288 + i * 6 + u] = jnp.where(
                odd, pltpu.roll(v, 16, 1), pltpu.roll(v, LANES - 16, 1)
            )
        return carry

    lax.fori_loop(0, BLK, swap, 0, unroll=2)
    for b in range(BLK):
        fetches[b].wait()
        if b + 2 < BLK:
            fetches[b + 2].start()
        patch(b, tbl_ref, table, st)
        at = slice(b * 32, b * 32 + 32)

        def load(j, at=at):
            return tuple(st[j, c, at, :] for c in range(4))

        values = lax.fori_loop(0, PASSES, lambda _, p, load=load: one_pass(load, p), start(load), unroll=6)
        for comp in range(4):
            params[comp, at, :] = values[comp]
    fine_slots(refine_ref, params, speed_ref, slots_ref)


def emit_kernel(meta_ref, params, planes_hbm, pf_ref, early_ref, late_ref, buffer, sem):
    def emit(b, carry):
        for comp in range(4):
            for xh in (0, 1):
                for yh in (0, 1):
                    buffer[pl.ds(b * 128 + 64 * xh + 4 * yh + comp, 8, stride=8), :] = params[
                        comp, pl.ds(b * 32 + yh * 16 + xh * 8, 8), :
                    ]
        return carry

    lax.fori_loop(0, BLK, emit, 0)
    copy = pltpu.make_async_copy(buffer, planes_hbm, sem)
    copy.start()
    plane_faces(params, pf_ref, BLK, 0)

    for todo_ref, first, parts in ((early_ref, 0, EARLY), (late_ref, EARLY, PARTS - EARLY)):

        def collect(i, n, todo_ref=todo_ref):
            todo_ref[n] = meta_ref[PARTS * SLOTS + i]
            return n + meta_ref[i]

        begin = first * SLOTS
        count = lax.fori_loop(begin, begin + parts * SLOTS, collect, 0, unroll=8)
        for extra in range(4):
            todo_ref[count + extra] = begin
        todo_ref[TODO - 1] = count
    copy.wait()


def moment_kernel(first, todo, pf_ref, speed_ref, *rest):
    *parts, out_ref, slots = rest
    lane = lane_ids()
    row = row_ids()
    if first == 0:
        out_ref[...] = jnp.zeros_like(out_ref)
    else:
        *parts, before_ref = parts
        out_ref[...] = before_ref[...]
    for at, ref in enumerate(parts):
        for u in range(12):
            slots[at * 12 + u] = ref[u]
    count = todo[TODO - 1]
    quarter = lane // 32
    first_off = (((lane // 16) % 2).astype(jnp.float32) - 0.5) * 0.5
    second_off = (((lane // 8) % 2).astype(jnp.float32) - 0.5) * 0.5

    def group(g, carry):
        fine = [None] * 3
        coarse = [None] * 5
        sign = None
        weight = None
        where = []

        def merge(old, new, q):
            return new if old is None else jnp.where(quarter == q, new, old)

        for q in range(4):
            at = 4 * g + q
            entry = todo[at]
            i = entry & 127
            c = lax.shift_right_logical(entry, 7) & 7
            k = lax.shift_right_logical(entry, 10) & 7
            quad = lax.shift_right_logical(entry, 13)
            axis = lax.shift_right_logical(k, 1)
            qa = lax.shift_right_logical(quad, 1)
            qb = quad & 1
            part = lax.shift_right_logical(i, 4) - first
            held = part * 12 + (lax.shift_right_logical(i, 2) & 3)
            turn = (i & 3) * 32 + lane % 32
            for comp in range(3):
                fine[comp] = merge(fine[comp], pick(slots[held + 4 * comp], turn), q)
            index = k * 16 + qb * 8 + lane % 8
            which = (axis, jnp.where(axis == 0, 1, 0), jnp.where(axis == 2, 1, 2), 3, 4)
            for at_comp, comp in enumerate(which):
                rows_at = pl.ds(pl.multiple_of(qa * 8, 8), 8)
                value = speed_ref[c, rows_at, :] if at_comp == 4 else pf_ref[c * 4 + comp, rows_at, :]
                coarse[at_comp] = merge(coarse[at_comp], pick(value, index), q)
            s = jnp.where((k & 1) == 1, -1.0, 1.0).astype(jnp.float32)
            sign = merge(sign, jnp.full((8, LANES), s, jnp.float32), q)
            on = jnp.where(at < count, 1.0, 0.0).astype(jnp.float32)
            weight = merge(weight, jnp.full((8, LANES), on, jnp.float32), q)
            where.append((((c * 6 + k) * 2 + qa) * 2, qb))
        an, df, uf = fine
        cn, t1, t2, dc, uc = coarse
        speed = sign * 0.5 * (uf + uc)
        depth = jnp.abs(speed) * TIME_STEP
        outflow = jnp.maximum(speed, 0.0)
        inflow = jnp.minimum(speed, 0.0)
        base = t1 * first_off + t2 * second_off + dc
        volume = 0.0
        moment = 0.0
        for node in NODES:
            fine_phase = an * (sign * (0.5 - node * depth)) + df
            coarse_phase = cn * (-sign * (0.5 - 0.5 * node * depth)) + base
            fine_model = 0.5 * (1.0 + jnp.tanh(fine_phase))
            coarse_model = 0.5 * (1.0 + jnp.tanh(coarse_phase))
            gain = outflow * fine_model
            loss = inflow * coarse_model
            volume = volume + 0.5 * TIME_STEP * (gain + loss)
            moment = moment + 0.5 * TIME_STEP * node * depth * sign * (loss - gain)
        sums = []
        for value in (volume * weight, moment * weight):
            value = value + pltpu.roll(value, LANES - 8, 1)
            sums.append(value + pltpu.roll(value, LANES - 16, 1))
        for q in range(4):
            target, qb = where[q]
            index = 32 * q + lane % 8
            keep = (lane // 16 == row) & ((lane // 8) % 2 == qb)
            rows = [
                jnp.sum(jnp.where(keep, pick(value, index), 0.0), axis=0, keepdims=True)
                for value in sums
            ]
            for m in range(2):
                out_ref[pl.ds(target + m, 1), :] = out_ref[pl.ds(target + m, 1), :] + rows[m]
        return carry

    lax.fori_loop(0, (count + 3) // 4, group, 0)


def partners(n, distance, offset):
    pairs = []
    for i in range(n):
        up = ((i - offset) // distance) % 2 == 0
        j = i + distance if up else i - distance
        pairs.append((i, j if 0 <= j < n else i ^ 1))
    return pairs


def trade(value):
    n = lax.axis_size("sfc")
    far = lax.ppermute(value, "sfc", partners(n, 2, 2))
    near = lax.ppermute(value, "sfc", partners(n, 2, 0))
    return [lax.ppermute(value, "sfc", partners(n, 1, 0)), near, far]


def relay(values):
    inside = partners(lax.axis_size("sfc"), 1, 0)
    return [lax.ppermute(value, "sfc", inside) for value in values]


def tiles(field):
    return field.reshape(BLK, 32, LANES).transpose(1, 0, 2).reshape(256, LANES)


def tiles3(field):
    return field.reshape(BLK, 3, 32, LANES).transpose(1, 2, 0, 3).reshape(3, 256, LANES)


def lasting(microseconds):
    return pl.CostEstimate(flops=0, transcendentals=0, bytes_accessed=microseconds * 3_500_000)


def per_device(fraction, centroid, velocity, neighbours, refinement):
    f32 = jnp.float32
    i32 = jnp.int32
    me = lax.axis_index("sfc").astype(i32)
    frac, cent, velo = tiles(fraction), tiles3(centroid), tiles3(velocity)
    out = functools.partial(jax.ShapeDtypeStruct, dtype=f32)
    limit = pltpu.CompilerParams(vmem_limit_bytes=12 << 20)

    hbm = pl.BlockSpec(memory_space=pltpu.HBM)
    faces, field, fine_rows, neighbours = pl.pallas_call(
        pack_kernel,
        out_shape=(
            out((49, 8, LANES)),
            out((4, 256, LANES)),
            jax.ShapeDtypeStruct((4, SLOTS), i32),
            jax.ShapeDtypeStruct((BLK, 6), i32),
        ),
        in_specs=[hbm] * 4,
        out_specs=(VMEM_SPEC,) * 4,
        scratch_shapes=[pltpu.SemaphoreType.DMA((6,))],
        compiler_params=limit,
        name="pack",
    )(*(pltpu.with_memory_space_constraint(v, pltpu.HBM) for v in (frac, cent, refinement.T, neighbours)))
    got = trade(faces)
    got = got + relay(got[1:])

    device = neighbours // BLK
    step = device // 2 - me // 2
    near_step = 1 - 2 * ((me // 2) % 2)
    part = jnp.where(
        step == 0,
        jnp.where(device == me, 0, 1),
        jnp.where(step == near_step, 2, 3) + jnp.where(device % 2 == me % 2, 0, 2),
    )
    direction = jnp.arange(6, dtype=i32)[None, :]
    block = jnp.arange(BLK, dtype=i32)[:, None]
    inside = part * BLK + neighbours % BLK
    x_row = jnp.where(neighbours >= 0, inside * 6 + 1 - direction, block * 6 + direction)
    yz_row = jnp.where(neighbours >= 0, inside, 48 + block) * 6 + 2
    rows = jnp.where(direction < 2, x_row, yz_row)
    rows = jnp.clip(rows, 0, 333).reshape(48)

    fine_local = jnp.clip(fine_rows[0] - me * BLK, 0, BLK - 1)
    fine_side = jnp.clip(fine_rows[1], 0, 5)
    fine_table = jnp.stack([fine_local, fine_side], axis=1).reshape(2 * SLOTS)

    points, speed = pl.pallas_call(
        prepare_kernel,
        out_shape=(pltpu.HBM((7, 4, 256, LANES), f32), out((BLK, 16, LANES))),
        in_specs=[VMEM_SPEC, hbm],
        out_specs=(hbm, VMEM_SPEC),
        scratch_shapes=[
            pltpu.VMEM((4, 2, 32, LANES), f32),
            pltpu.VMEM((7, 4, 256, LANES), f32),
            pltpu.VMEM((3, 256, LANES), f32),
            pltpu.SemaphoreType.DMA,
            pltpu.SemaphoreType.DMA,
        ],
        compiler_params=limit,
        cost_estimate=lasting(4),
        name="prepare",
    )(field, pltpu.with_memory_space_constraint(velo, pltpu.HBM))
    points = pltpu.with_memory_space_constraint(points, pltpu.HBM)
    params, slots = pl.pallas_call(
        fit_kernel,
        out_shape=(out((4, 256, LANES)), out((12, 8, LANES))),
        in_specs=[SMEM_SPEC] * 2 + [VMEM_SPEC] * 6 + [hbm, VMEM_SPEC],
        out_specs=(VMEM_SPEC,) * 2,
        scratch_shapes=[
            pltpu.VMEM((7, 4, 256, LANES), f32),
            pltpu.VMEM((336, 8, LANES), f32),
            pltpu.SemaphoreType.DMA((BLK,)),
        ],
        compiler_params=limit,
        cost_estimate=lasting(12),
        name="fit",
    )(rows, fine_table, faces, *got, points, speed)
    got_slots = trade(slots)

    count = lax.axis_size("sfc")
    twice = (me // 2 == 0) | (me // 2 == count // 2 - 1)
    tables = jnp.stack(
        [fine_rows] + [v[48, 0:4, 0:SLOTS].astype(i32) for v in got], axis=1
    )
    part_ids = jnp.arange(PARTS, dtype=i32)[:, None]
    fresh = jnp.logical_not(twice & ((part_ids == 3) | (part_ids == 5)))
    mine = (tables[0] >= 0) & (tables[2] // BLK == me) & fresh
    side = jnp.clip(tables[1], 0, 5)
    slot_ids = jnp.arange(PARTS * SLOTS, dtype=i32).reshape(PARTS, SLOTS)
    entry = (
        slot_ids
        + 128 * (jnp.clip(tables[2], 0, None) % BLK)
        + 1024 * (side + 1 - 2 * (side % 2))
        + 8192 * jnp.clip(tables[3], 0, 3)
    )
    meta = jnp.stack([mine.astype(i32), entry]).reshape(2 * PARTS * SLOTS)

    todo = jax.ShapeDtypeStruct((TODO,), i32)
    planes, plane_face, early, late = pl.pallas_call(
        emit_kernel,
        out_shape=(out((1024, LANES)), out((BLK * 4, 16, LANES)), todo, todo),
        in_specs=[SMEM_SPEC, VMEM_SPEC],
        out_specs=(hbm, VMEM_SPEC, SMEM_SPEC, SMEM_SPEC),
        scratch_shapes=[pltpu.VMEM((1024, LANES), f32), pltpu.SemaphoreType.DMA],
        compiler_params=limit,
        cost_estimate=lasting(2),
        name="emit",
    )(meta, params)
    plane_face, near, far = lax.optimization_barrier((plane_face, *got_slots[1:]))
    others = relay([near, far])

    def moments(first, todo, *operands):
        return pl.pallas_call(
            functools.partial(moment_kernel, first),
            out_shape=out((BLK * 6 * 4, LANES)),
            in_specs=[SMEM_SPEC] + [VMEM_SPEC] * (2 + len(operands)),
            out_specs=VMEM_SPEC,
            scratch_shapes=[pltpu.VMEM((EARLY * 12, 8, LANES), f32)],
            compiler_params=limit,
            cost_estimate=lasting(2),
            name="moments",
        )(todo, plane_face, speed, *operands)

    reflux = moments(0, early, slots, got_slots[0], near, far)
    reflux = moments(EARLY, late, *others, reflux)

    planes = planes.reshape(BLK, 32, 4, LANES).transpose(0, 2, 1, 3).reshape(BLK, 4, 4096)
    reflux = reflux.reshape(BLK, 6, 2, 2, LANES).transpose(0, 1, 3, 2, 4).reshape(BLK, 6, 2, 256)
    return planes, reflux


def solution(mesh):
    return jax.shard_map(
        per_device,
        mesh=mesh,
        in_specs=(
            P("sfc", None),
            P("sfc", None, None),
            P("sfc", None, None),
            P("sfc", None),
            P("sfc", None),
        ),
        out_specs=(P("sfc", None, None), P("sfc", None, None, None)),
        check_vma=False,
    )
```

```python
import functools

import jax
import jax.numpy as jnp
from jax import lax
from jax.experimental import pallas as pl
from jax.experimental.pallas import tpu as pltpu
from jax.sharding import PartitionSpec as P

BLK = 8
SLOTS = 16
PARTS = 6
TODO = 112
EARLY = 4
PASSES = 6
LANES = 128
NODES = (0.5 - 3.0**0.5 / 6.0, 0.5 + 3.0**0.5 / 6.0)
TIME_STEP = 0.25
DAMPING = 0.1
VMEM_SPEC = pl.BlockSpec(memory_space=pltpu.VMEM)
SMEM_SPEC = pl.BlockSpec(memory_space=pltpu.SMEM)


def lane_ids():
    return lax.broadcasted_iota(jnp.int32, (8, LANES), 1)


def row_ids():
    return lax.broadcasted_iota(jnp.int32, (8, LANES), 0)


def pick(values, index):
    return jnp.take_along_axis(values, index, axis=1, mode="promise_in_bounds")


def cells(ref, b, xh, yh):
    return ref[pl.ds(xh * 128 + yh * 8 + b, 8, stride=16), :]


def side_index(lane):
    l = lane % 64
    index = jnp.where(l < 16, l, jnp.where(l < 32, l + 96, 16 * (l % 8) + jnp.where(l < 48, 0, 15)))
    upper = ((l >= 16) & (l < 32)) | ((l >= 40) & (l < 48)) | (l >= 56)
    return index, upper


def pack_kernel(
    frac_hbm, cent_hbm, refine_hbm, near_hbm, out_ref, field, refine_ref, near_ref, sems
):
    copies = [
        pltpu.make_async_copy(frac_hbm if f == 0 else cent_hbm.at[f - 1], field.at[f], sems.at[f])
        for f in range(4)
    ]
    copies.append(pltpu.make_async_copy(refine_hbm, refine_ref, sems.at[4]))
    copies.append(pltpu.make_async_copy(near_hbm, near_ref, sems.at[5]))
    for copy in copies:
        copy.start()
    lane = lane_ids()
    index, upper = side_index(lane)
    out_ref[48] = jnp.zeros((8, LANES), jnp.float32)
    for fp in (0, 1):

        def block(b, carry, fp=fp):
            for xh in (0, 1):
                sides = []
                for f in (2 * fp, 2 * fp + 1):
                    half = [cells(field.at[f], b, xh, yh) for yh in (0, 1)]
                    for yh in (0, 1):
                        row = half[yh][0:1] if xh == 0 else half[yh][7:8]
                        out_ref[b * 6 + xh, 2 * f + yh : 2 * f + yh + 1, :] = row
                    sides.append(jnp.where(upper, pick(half[1], index), pick(half[0], index)))
                out_ref[b * 6 + 2 + 2 * fp + xh] = jnp.where(lane < 64, sides[0], sides[1])
            return carry

        copies[2 * fp].wait()
        copies[2 * fp + 1].wait()
        lax.fori_loop(0, BLK, block, 0, unroll=4)
    for copy in copies[4:]:
        copy.wait()
    out_ref[48, 0:4, 0:SLOTS] = refine_ref[...].astype(jnp.float32)


def solve(h, g):
    a, b, c = h[0][0], h[0][1], h[1][1]
    ra = 1.0 / (a * c - b * b)
    ia, ib, ic = c * ra, b * ra, a * ra
    p, q, r, s = h[0][2], h[0][3], h[1][2], h[1][3]
    wp, wq = ia * p - ib * r, ia * q - ib * s
    wr, ws = ic * r - ib * p, ic * s - ib * q
    sa = h[2][2] - p * wp - r * wr
    sb = h[2][3] - p * wq - r * ws
    sc = h[3][3] - q * wq - s * ws
    z0, z1 = ia * g[0] - ib * g[1], ic * g[1] - ib * g[0]
    y0 = g[2] - p * z0 - r * z1
    y1 = g[3] - q * z0 - s * z1
    rs = 1.0 / (sa * sc - sb * sb)
    x2 = (sc * y0 - sb * y1) * rs
    x3 = (sa * y1 - sb * y0) * rs
    return z0 - wp * x2 - wq * x3, z1 - wr * x2 - ws * x3, x2, x3


def one_pass(load, params):
    a, b, c, d = params
    h = [[None] * 4 for _ in range(4)]
    g = [None] * 4

    def add(total, value):
        return value if total is None else total + value

    for j in range(7):
        px, py, pz, q = load(j)
        t = jnp.tanh(a * px + b * py + c * pz + d)
        s = 1.0 - t * t
        w = s * s
        r = s * (t + q)
        wx, wy, wz = w * px, w * py, w * pz
        h[0][0] = add(h[0][0], wx * px)
        h[0][1] = add(h[0][1], wx * py)
        h[0][2] = add(h[0][2], wx * pz)
        h[0][3] = add(h[0][3], wx)
        h[1][1] = add(h[1][1], wy * py)
        h[1][2] = add(h[1][2], wy * pz)
        h[1][3] = add(h[1][3], wy)
        h[2][2] = add(h[2][2], wz * pz)
        h[2][3] = add(h[2][3], wz)
        h[3][3] = add(h[3][3], w)
        g[0] = add(g[0], r * px)
        g[1] = add(g[1], r * py)
        g[2] = add(g[2], r * pz)
        g[3] = add(g[3], r)
    for i in range(4):
        h[i][i] = h[i][i] + 4.0 * DAMPING
    step = solve(h, g)
    return tuple(p - u for p, u in zip(params, step))


def start(load):
    f = [0.5 - 0.5 * load(j)[3] for j in range(7)]
    cx, cy, cz, _ = load(0)
    a, b, c = (2.0 * (f[2 * k + 2] - f[2 * k + 1]) for k in range(3))
    d = 2.0 * (2.0 * f[0] - 1.0) - a * cx - b * cy - c * cz
    return a, b, c, d


def held_as(f, j, value):
    if f == 0:
        return 1.0 - 2.0 * value
    if j > 0 and (j - 1) // 2 == f - 1:
        return value + (1.0 if (j - 1) % 2 else -1.0)
    return value


def own_points(field, xpad, st):
    lane = lane_ids()

    def block(b, carry):
        for f in range(4):

            def put(j, xh, yh, value):
                at = pl.ds(b * 32 + yh * 16 + xh * 8, 8)
                st[j, (f + 3) % 4, at, :] = held_as(f, j, value)

            own = [[cells(field.at[f], b, xh, yh) for yh in (0, 1)] for xh in (0, 1)]
            for yh in (0, 1):
                for xh in (0, 1):
                    xpad[f, yh, 8 + 8 * xh : 16 + 8 * xh, :] = own[xh][yh]
            for xh in (0, 1):
                up = [pltpu.roll(own[xh][yh], 16, 1) for yh in (0, 1)]
                down = [pltpu.roll(own[xh][yh], LANES - 16, 1) for yh in (0, 1)]
                for yh in (0, 1):
                    mine = own[xh][yh]
                    put(0, xh, yh, mine)
                    put(1, xh, yh, xpad[f, yh, 7 + 8 * xh : 15 + 8 * xh, :])
                    put(2, xh, yh, xpad[f, yh, 9 + 8 * xh : 17 + 8 * xh, :])
                    put(3, xh, yh, up[0] if yh == 0 else jnp.where(lane < 16, up[0], up[1]))
                    put(4, xh, yh, down[1] if yh == 1 else jnp.where(lane >= 112, down[1], down[0]))
                    put(5, xh, yh, pltpu.roll(mine, 1, 1))
                    put(6, xh, yh, pltpu.roll(mine, LANES - 1, 1))
        return carry

    xpad[...] = jnp.zeros_like(xpad)
    lax.fori_loop(0, BLK, block, 0)


def patch(b, tbl_ref, table, st):
    lane = lane_ids()
    group = (lane % 64) // 16
    src = [tbl_ref[b * 6 + k] for k in range(6)]
    low, high = table[src[0]], table[src[1]]

    def put(j, f, at, mask, value):
        c = (f + 3) % 4
        st[j, c, at, :] = jnp.where(mask, held_as(f, j, value), st[j, c, at, :])

    for f in range(4):
        c = (f + 3) % 4
        for yh in (0, 1):
            row = b * 32 + yh * 16
            st[1, c, row : row + 1, :] = held_as(f, 1, low[2 * f + yh : 2 * f + yh + 1])
            st[2, c, row + 15 : row + 16, :] = held_as(f, 2, high[2 * f + yh : 2 * f + yh + 1])
    for fp in (0, 1):
        for xh in (0, 1):
            ghost = [table[src[k] + 2 * fp + xh] for k in range(2, 6)]
            mixed = jnp.where(
                group < 2,
                jnp.where(group == 0, ghost[1], ghost[0]),
                jnp.where(group == 2, ghost[3], ghost[2]),
            )
            for fh in (0, 1):
                f = 2 * fp + fh
                for yh in (0, 1):
                    row = b * 32 + yh * 16 + xh * 8
                    at = slice(row, row + 8)
                    index = fh * 64 + jnp.where(lane % 16 == 15, 32, 48) + yh * 8 + lane // 16
                    value = pick(mixed, index)
                    put(5, f, at, lane % 16 == 0, value)
                    put(6, f, at, lane % 16 == 15, value)
                    value = pick(mixed, fh * 64 + (16 if yh == 0 else 0) + lane % 16)
                    if yh == 0:
                        put(3, f, at, lane < 16, value)
                    else:
                        put(4, f, at, lane >= 112, value)


def face_index(lane):
    index = jnp.where(
        lane < 48,
        lane % 16,
        jnp.where(lane < 64, lane + 64, 16 * (lane % 8) + jnp.where(lane < 80, 0, 15)),
    )
    upper = (
        ((lane >= 48) & (lane < 64)) | ((lane >= 72) & (lane < 80)) | ((lane >= 88) & (lane < 96))
    )
    return index, upper


def x_faces(lane, row, first, h):
    unroll_x = row * 16 + lane % 16
    low = pick(jnp.broadcast_to(first[0][h][0:1], (8, LANES)), unroll_x)
    high = pick(jnp.broadcast_to(first[1][h][7:8], (8, LANES)), unroll_x)
    return low, high


def prepare_kernel(field, velo_hbm, points_hbm, out_ref, xpad, st, velo_ref, sem, velo_sem):
    fetch = pltpu.make_async_copy(velo_hbm, velo_ref, velo_sem)
    fetch.start()
    own_points(field, xpad, st)
    keep = pltpu.make_async_copy(st, points_hbm, sem)
    keep.start()
    fetch.wait()
    lane, row = lane_ids(), row_ids()
    index, upper = face_index(lane)

    def block(b, carry):
        x, y, z = (
            [[cells(velo_ref.at[axis], b, xh, yh) for yh in (0, 1)] for xh in (0, 1)]
            for axis in range(3)
        )
        for h in (0, 1):
            low, high = x_faces(lane, row, x, h)
            y_sides = jnp.where(upper, pick(y[h][1], index), pick(y[h][0], index))
            z_sides = jnp.where(upper, pick(z[h][1], index), pick(z[h][0], index))
            sides = jnp.where(lane < 64, y_sides, z_sides)
            out_ref[b, 8 * h : 8 * h + 8, :] = jnp.where(
                lane < 16, low, jnp.where(lane < 32, high, sides)
            )
        return carry

    lax.fori_loop(0, BLK, block, 0, unroll=2)
    keep.wait()


def plane_faces(params, pf, count, first):
    lane, row = lane_ids(), row_ids()
    index, upper = face_index(lane)

    def block(b, carry):
        for comp in range(4):
            value = [
                [params[comp, pl.ds(b * 32 + yh * 16 + xh * 8, 8), :] for yh in (0, 1)]
                for xh in (0, 1)
            ]
            for h in (0, 1):
                low, high = x_faces(lane, row, value, h)
                sides = jnp.where(upper, pick(value[h][1], index), pick(value[h][0], index))
                pf[(first + b) * 4 + comp, 8 * h : 8 * h + 8, :] = jnp.where(
                    lane < 16, low, jnp.where(lane < 32, high, sides)
                )
        return carry

    lax.fori_loop(0, count, block, 0, unroll=2)


def fine_slots(refine_ref, params, speed_ref, slots_ref):
    lane, row = lane_ids(), row_ids()
    isub = (lane // 16) % 2
    odd = isub == 1
    second = 2 * (lane % 8) + (lane // 8) % 2
    x_source = 16 * ((2 * row + isub) % 8) + second

    def tile(g, carry):
        total = [None] * 3
        for q in range(4):
            f = refine_ref[2 * (4 * g + q)]
            k = refine_ref[2 * (4 * g + q) + 1]
            axis = lax.shift_right_logical(k, 1)
            side = k & 1
            y_source = side * 112 + second
            z_source = 16 * (second % 8) + 15 * side
            is_x = jnp.full((8, LANES), axis, jnp.int32) == 0
            is_y = jnp.full((8, LANES), axis, jnp.int32) == 1
            upper = second >= 8
            got = []
            for comp in (axis, 3):
                at = f * 32
                ref = params.at[comp]
                line = at + side * 15
                x_value = pick(
                    jnp.where(
                        row < 4,
                        jnp.broadcast_to(ref[pl.ds(line, 1), :], (8, LANES)),
                        jnp.broadcast_to(ref[pl.ds(line + 16, 1), :], (8, LANES)),
                    ),
                    x_source,
                )
                part = [
                    [ref[pl.ds(at + 16 * yh + sub, 8, stride=2), :] for yh in (0, 1)]
                    for sub in (0, 1)
                ]
                high_side = jnp.full((8, LANES), side, jnp.int32) == 1
                y_part = [pick(jnp.where(high_side, p[1], p[0]), y_source) for p in part]
                z_part = [jnp.where(upper, pick(p[1], z_source), pick(p[0], z_source)) for p in part]
                got.append(
                    jnp.where(
                        is_x,
                        x_value,
                        jnp.where(
                            is_y,
                            jnp.where(odd, y_part[1], y_part[0]),
                            jnp.where(odd, z_part[1], z_part[0]),
                        ),
                    )
                )
            index = k * 16 + second
            got.append(
                jnp.where(
                    odd,
                    pick(speed_ref[f, pl.ds(1, 8, stride=2), :], index),
                    pick(speed_ref[f, pl.ds(0, 8, stride=2), :], index),
                )
            )
            for comp in range(3):
                old = total[comp]
                total[comp] = got[comp] if q == 0 else jnp.where(lane // 32 == q, got[comp], old)
        for comp in range(3):
            slots_ref[4 * comp + g] = total[comp]
        return carry

    lax.fori_loop(0, SLOTS // 4, tile, 0, unroll=True)


def fit_kernel(
    tbl_ref, refine_ref, own_ref, r1_ref, r2_ref, r3_ref, r4_ref, r5_ref, points_hbm, speed_ref,
    params, slots_ref, st, table, sems,
):
    fetches = [
        pltpu.make_async_copy(
            points_hbm.at[:, :, pl.ds(b * 32, 32), :], st.at[:, :, pl.ds(b * 32, 32), :], sems.at[b]
        )
        for b in range(BLK)
    ]
    fetches[0].start()
    fetches[1].start()
    lane = lane_ids()
    for at, ref in enumerate((own_ref, r1_ref, r2_ref, r3_ref, r4_ref, r5_ref)):

        def copy(i, carry, at=at, ref=ref):
            for u in range(12):
                table[at * 48 + i * 12 + u] = ref[i * 12 + u]
            return carry

        lax.fori_loop(0, 4, copy, 0, unroll=True)

    def swap(i, carry):
        for u in range(2, 6):
            v = own_ref[i * 6 + u]
            odd = (lane // 16) % 2 == 1
            table[288 + i * 6 + u] = jnp.where(
                odd, pltpu.roll(v, 16, 1), pltpu.roll(v, LANES - 16, 1)
            )
        return carry

    lax.fori_loop(0, BLK, swap, 0, unroll=True)
    for b in range(BLK):
        fetches[b].wait()
        if b + 2 < BLK:
            fetches[b + 2].start()
        patch(b, tbl_ref, table, st)
        at = slice(b * 32, b * 32 + 32)

        def load(j, at=at):
            return tuple(st[j, c, at, :] for c in range(4))

        values = lax.fori_loop(0, PASSES, lambda _, p, load=load: one_pass(load, p), start(load), unroll=6)
        for comp in range(4):
            params[comp, at, :] = values[comp]
    fine_slots(refine_ref, params, speed_ref, slots_ref)


def emit_kernel(meta_ref, params, planes_hbm, pf_ref, early_ref, late_ref, buffer, sem):
    def emit(b, carry):
        for comp in range(4):
            for xh in (0, 1):
                for yh in (0, 1):
                    buffer[pl.ds(b * 128 + 64 * xh + 4 * yh + comp, 8, stride=8), :] = params[
                        comp, pl.ds(b * 32 + yh * 16 + xh * 8, 8), :
                    ]
        return carry

    lax.fori_loop(0, BLK, emit, 0)
    copy = pltpu.make_async_copy(buffer, planes_hbm, sem)
    copy.start()
    plane_faces(params, pf_ref, BLK, 0)

    for todo_ref, first, parts in ((early_ref, 0, EARLY), (late_ref, EARLY, PARTS - EARLY)):

        def collect(i, n, todo_ref=todo_ref):
            todo_ref[n] = meta_ref[PARTS * SLOTS + i]
            return n + meta_ref[i]

        begin = first * SLOTS
        count = lax.fori_loop(begin, begin + parts * SLOTS, collect, 0, unroll=8)
        for extra in range(4):
            todo_ref[count + extra] = begin
        todo_ref[TODO - 1] = count
    copy.wait()


def moment_kernel(first, todo, pf_ref, speed_ref, *rest):
    *parts, out_ref, slots = rest
    lane = lane_ids()
    row = row_ids()
    if first == 0:
        out_ref[...] = jnp.zeros_like(out_ref)
    else:
        *parts, before_ref = parts
        out_ref[...] = before_ref[...]
    for at, ref in enumerate(parts):
        for u in range(12):
            slots[at * 12 + u] = ref[u]
    count = todo[TODO - 1]
    quarter = lane // 32
    first_off = (((lane // 16) % 2).astype(jnp.float32) - 0.5) * 0.5
    second_off = (((lane // 8) % 2).astype(jnp.float32) - 0.5) * 0.5

    def group(g, carry):
        fine = [None] * 3
        coarse = [None] * 5
        sign = None
        weight = None
        where = []

        def merge(old, new, q):
            return new if old is None else jnp.where(quarter == q, new, old)

        for q in range(4):
            at = 4 * g + q
            entry = todo[at]
            i = entry & 127
            c = lax.shift_right_logical(entry, 7) & 7
            k = lax.shift_right_logical(entry, 10) & 7
            quad = lax.shift_right_logical(entry, 13)
            axis = lax.shift_right_logical(k, 1)
            qa = lax.shift_right_logical(quad, 1)
            qb = quad & 1
            part = lax.shift_right_logical(i, 4) - first
            held = part * 12 + (lax.shift_right_logical(i, 2) & 3)
            turn = (i & 3) * 32 + lane % 32
            for comp in range(3):
                fine[comp] = merge(fine[comp], pick(slots[held + 4 * comp], turn), q)
            index = k * 16 + qb * 8 + lane % 8
            which = (axis, jnp.where(axis == 0, 1, 0), jnp.where(axis == 2, 1, 2), 3, 4)
            for at_comp, comp in enumerate(which):
                rows_at = pl.ds(pl.multiple_of(qa * 8, 8), 8)
                value = speed_ref[c, rows_at, :] if at_comp == 4 else pf_ref[c * 4 + comp, rows_at, :]
                coarse[at_comp] = merge(coarse[at_comp], pick(value, index), q)
            s = jnp.where((k & 1) == 1, -1.0, 1.0).astype(jnp.float32)
            sign = merge(sign, jnp.full((8, LANES), s, jnp.float32), q)
            on = jnp.where(at < count, 1.0, 0.0).astype(jnp.float32)
            weight = merge(weight, jnp.full((8, LANES), on, jnp.float32), q)
            where.append((((c * 6 + k) * 2 + qa) * 2, qb))
        an, df, uf = fine
        cn, t1, t2, dc, uc = coarse
        speed = sign * 0.5 * (uf + uc)
        depth = jnp.abs(speed) * TIME_STEP
        outflow = jnp.maximum(speed, 0.0)
        inflow = jnp.minimum(speed, 0.0)
        base = t1 * first_off + t2 * second_off + dc
        volume = 0.0
        moment = 0.0
        for node in NODES:
            fine_phase = an * (sign * (0.5 - node * depth)) + df
            coarse_phase = cn * (-sign * (0.5 - 0.5 * node * depth)) + base
            fine_model = 0.5 * (1.0 + jnp.tanh(fine_phase))
            coarse_model = 0.5 * (1.0 + jnp.tanh(coarse_phase))
            gain = outflow * fine_model
            loss = inflow * coarse_model
            volume = volume + 0.5 * TIME_STEP * (gain + loss)
            moment = moment + 0.5 * TIME_STEP * node * depth * sign * (loss - gain)
        sums = []
        for value in (volume * weight, moment * weight):
            value = value + pltpu.roll(value, LANES - 8, 1)
            sums.append(value + pltpu.roll(value, LANES - 16, 1))
        for q in range(4):
            target, qb = where[q]
            index = 32 * q + lane % 8
            keep = (lane // 16 == row) & ((lane // 8) % 2 == qb)
            rows = [
                jnp.sum(jnp.where(keep, pick(value, index), 0.0), axis=0, keepdims=True)
                for value in sums
            ]
            for m in range(2):
                out_ref[pl.ds(target + m, 1), :] = out_ref[pl.ds(target + m, 1), :] + rows[m]
        return carry

    lax.fori_loop(0, (count + 3) // 4, group, 0)


def partners(n, distance, offset):
    pairs = []
    for i in range(n):
        up = ((i - offset) // distance) % 2 == 0
        j = i + distance if up else i - distance
        pairs.append((i, j if 0 <= j < n else i ^ 1))
    return pairs


def trade(value):
    n = lax.axis_size("sfc")
    far = lax.ppermute(value, "sfc", partners(n, 2, 2))
    near = lax.ppermute(value, "sfc", partners(n, 2, 0))
    return [lax.ppermute(value, "sfc", partners(n, 1, 0)), near, far]


def relay(values):
    inside = partners(lax.axis_size("sfc"), 1, 0)
    return [lax.ppermute(value, "sfc", inside) for value in values]


def tiles(field):
    return field.reshape(BLK, 32, LANES).transpose(1, 0, 2).reshape(256, LANES)


def tiles3(field):
    return field.reshape(BLK, 3, 32, LANES).transpose(1, 2, 0, 3).reshape(3, 256, LANES)


def lasting(microseconds):
    return pl.CostEstimate(flops=0, transcendentals=0, bytes_accessed=microseconds * 3_500_000)


def per_device(fraction, centroid, velocity, neighbours, refinement):
    f32 = jnp.float32
    i32 = jnp.int32
    me = lax.axis_index("sfc").astype(i32)
    frac, cent, velo = tiles(fraction), tiles3(centroid), tiles3(velocity)
    out = functools.partial(jax.ShapeDtypeStruct, dtype=f32)
    limit = pltpu.CompilerParams(vmem_limit_bytes=12 << 20)

    hbm = pl.BlockSpec(memory_space=pltpu.HBM)
    faces, field, fine_rows, neighbours = pl.pallas_call(
        pack_kernel,
        out_shape=(
            out((49, 8, LANES)),
            out((4, 256, LANES)),
            jax.ShapeDtypeStruct((4, SLOTS), i32),
            jax.ShapeDtypeStruct((BLK, 6), i32),
        ),
        in_specs=[hbm] * 4,
        out_specs=(VMEM_SPEC,) * 4,
        scratch_shapes=[pltpu.SemaphoreType.DMA((6,))],
        compiler_params=limit,
        name="pack",
    )(*(pltpu.with_memory_space_constraint(v, pltpu.HBM) for v in (frac, cent, refinement.T, neighbours)))
    got = trade(faces)
    got = got + relay(got[1:])

    device = neighbours // BLK
    step = device // 2 - me // 2
    near_step = 1 - 2 * ((me // 2) % 2)
    part = jnp.where(
        step == 0,
        jnp.where(device == me, 0, 1),
        jnp.where(step == near_step, 2, 3) + jnp.where(device % 2 == me % 2, 0, 2),
    )
    direction = jnp.arange(6, dtype=i32)[None, :]
    block = jnp.arange(BLK, dtype=i32)[:, None]
    inside = part * BLK + neighbours % BLK
    x_row = jnp.where(neighbours >= 0, inside * 6 + 1 - direction, block * 6 + direction)
    yz_row = jnp.where(neighbours >= 0, inside, 48 + block) * 6 + 2
    rows = jnp.where(direction < 2, x_row, yz_row)
    rows = jnp.clip(rows, 0, 333).reshape(48)

    fine_local = jnp.clip(fine_rows[0] - me * BLK, 0, BLK - 1)
    fine_side = jnp.clip(fine_rows[1], 0, 5)
    fine_table = jnp.stack([fine_local, fine_side], axis=1).reshape(2 * SLOTS)

    points, speed = pl.pallas_call(
        prepare_kernel,
        out_shape=(pltpu.HBM((7, 4, 256, LANES), f32), out((BLK, 16, LANES))),
        in_specs=[VMEM_SPEC, hbm],
        out_specs=(hbm, VMEM_SPEC),
        scratch_shapes=[
            pltpu.VMEM((4, 2, 32, LANES), f32),
            pltpu.VMEM((7, 4, 256, LANES), f32),
            pltpu.VMEM((3, 256, LANES), f32),
            pltpu.SemaphoreType.DMA,
            pltpu.SemaphoreType.DMA,
        ],
        compiler_params=limit,
        cost_estimate=lasting(4),
        name="prepare",
    )(field, pltpu.with_memory_space_constraint(velo, pltpu.HBM))
    points = pltpu.with_memory_space_constraint(points, pltpu.HBM)
    params, slots = pl.pallas_call(
        fit_kernel,
        out_shape=(out((4, 256, LANES)), out((12, 8, LANES))),
        in_specs=[SMEM_SPEC] * 2 + [VMEM_SPEC] * 6 + [hbm, VMEM_SPEC],
        out_specs=(VMEM_SPEC,) * 2,
        scratch_shapes=[
            pltpu.VMEM((7, 4, 256, LANES), f32),
            pltpu.VMEM((336, 8, LANES), f32),
            pltpu.SemaphoreType.DMA((BLK,)),
        ],
        compiler_params=limit,
        cost_estimate=lasting(12),
        name="fit",
    )(rows, fine_table, faces, *got, points, speed)
    got_slots = trade(slots)

    count = lax.axis_size("sfc")
    twice = (me // 2 == 0) | (me // 2 == count // 2 - 1)
    tables = jnp.stack(
        [fine_rows] + [v[48, 0:4, 0:SLOTS].astype(i32) for v in got], axis=1
    )
    part_ids = jnp.arange(PARTS, dtype=i32)[:, None]
    fresh = jnp.logical_not(twice & ((part_ids == 3) | (part_ids == 5)))
    mine = (tables[0] >= 0) & (tables[2] // BLK == me) & fresh
    side = jnp.clip(tables[1], 0, 5)
    slot_ids = jnp.arange(PARTS * SLOTS, dtype=i32).reshape(PARTS, SLOTS)
    entry = (
        slot_ids
        + 128 * (jnp.clip(tables[2], 0, None) % BLK)
        + 1024 * (side + 1 - 2 * (side % 2))
        + 8192 * jnp.clip(tables[3], 0, 3)
    )
    meta = jnp.stack([mine.astype(i32), entry]).reshape(2 * PARTS * SLOTS)

    todo = jax.ShapeDtypeStruct((TODO,), i32)
    planes, plane_face, early, late = pl.pallas_call(
        emit_kernel,
        out_shape=(out((1024, LANES)), out((BLK * 4, 16, LANES)), todo, todo),
        in_specs=[SMEM_SPEC, VMEM_SPEC],
        out_specs=(hbm, VMEM_SPEC, SMEM_SPEC, SMEM_SPEC),
        scratch_shapes=[pltpu.VMEM((1024, LANES), f32), pltpu.SemaphoreType.DMA],
        compiler_params=limit,
        cost_estimate=lasting(2),
        name="emit",
    )(meta, params)
    plane_face, near, far = lax.optimization_barrier((plane_face, *got_slots[1:]))
    others = relay([near, far])

    def moments(first, todo, *operands):
        return pl.pallas_call(
            functools.partial(moment_kernel, first),
            out_shape=out((BLK * 6 * 4, LANES)),
            in_specs=[SMEM_SPEC] + [VMEM_SPEC] * (2 + len(operands)),
            out_specs=VMEM_SPEC,
            scratch_shapes=[pltpu.VMEM((EARLY * 12, 8, LANES), f32)],
            compiler_params=limit,
            cost_estimate=lasting(2),
            name="moments",
        )(todo, plane_face, speed, *operands)

    reflux = moments(0, early, slots, got_slots[0], near, far)
    reflux = moments(EARLY, late, *others, reflux)

    planes = planes.reshape(BLK, 32, 4, LANES).transpose(0, 2, 1, 3).reshape(BLK, 4, 4096)
    reflux = reflux.reshape(BLK, 6, 2, 2, LANES).transpose(0, 1, 3, 2, 4).reshape(BLK, 6, 2, 256)
    return planes, reflux


def solution(mesh):
    return jax.shard_map(
        per_device,
        mesh=mesh,
        in_specs=(
            P("sfc", None),
            P("sfc", None, None),
            P("sfc", None, None),
            P("sfc", None),
            P("sfc", None),
        ),
        out_specs=(P("sfc", None, None), P("sfc", None, None, None)),
        check_vma=False,
    )
```
